512 devices in a mesh: term: 8 (over z), sector: 64 (over x, y, core).
Axes of the slice: x: 4, y: 8, z: 8, core: 2. Of those that a mesh axis runs over, the one named last changes fastest.
Arguments:
- wave_tiles: bfloat16 [1024, 2, 128, 128], P('sector'), may hold values from -6 to 6
- left_env: bfloat16 [8, 64, 128, 128], P('term', 'sector'), may hold values from -0.5 to 0.5
- right_env: bfloat16 [8, 64, 128, 128], P('term', 'sector'), may hold values from -0.5 to 0.5
- send_list: int32 [64, 128], P('sector'), may hold values from -1 to 15, as said below
- left_tasks: int32 [8, 64, 96, 3], P('term', 'sector'), may hold values from 0 to 127, as said below
- right_tasks: int32 [8, 64, 256, 3], P('term', 'sector'), may hold values from 0 to 63, as said below
Outputs:
- sigma: float32 [1024, 2, 128, 128], P('sector', None, 'term')
The draws below stay inside these ranges and needn't reach their ends.
Inputs may be any that keep to these rules, and one draw needn't show every extreme that they name: send_list[s, o * 2 + c] is a tile index local to sender s, or -1 for an empty slot; some owner drawn from the seed receives a full 2 tiles from every sender. `left_tasks`: entries 0, 1, 2 lie below 64, 128 and 32. `right_tasks`: entries 0, 1, 2 lie below 32, 64 and 16.
All inputs are finite; a program needn't handle non-finite values.
Results may differ from the reference program's by a relative error of at most 0.0029.
Values may be sent and summed in bfloat16 or wider, within the bound.
A program may use at most 128 MiB of HBM per device.

```python
import jax
import jax.numpy as jnp
from jax import lax

TILE_DIM = 128
VECTORS = 2
CAPACITY = 2
TILE_DEV = 16
LEFT_TASKS = 96
RIGHT_TASKS = 256
INTER_TILES = 32
OWNERS = 64
GROUPS = 8
SEND_SLOTS = 128
ENV_TILES = 64
ALL_TILES = 1024


def draw_send_list(key, part):
    key_weight, key_live, key_full, key_index = jax.random.split(key, 4)
    weights = jax.random.randint(key_weight, (OWNERS,), 3, 8)
    rolls = jax.random.randint(key_live, (OWNERS, OWNERS, CAPACITY), 0, 8)
    live = rolls < weights[None, :, None]
    full_owner = jax.random.randint(key_full, (), 0, OWNERS)
    live = live | (jnp.arange(OWNERS) == full_owner)[None, :, None]
    index = jax.random.randint(key_index, (OWNERS, OWNERS, CAPACITY), 0, TILE_DEV)
    return jnp.where(live, index, -1).reshape(OWNERS, SEND_SLOTS).astype(jnp.int32)


def draw_left_tasks(key, part):
    key_env, key_slot, key_inter = jax.random.split(key, 3)
    shape = (GROUPS, OWNERS, LEFT_TASKS)
    columns = [jax.random.randint(key_env, shape, 0, ENV_TILES), jax.random.randint(key_slot, shape, 0, SEND_SLOTS), jax.random.randint(key_inter, shape, 0, INTER_TILES)]
    return jnp.stack(columns, axis=-1).astype(jnp.int32)


def draw_right_tasks(key, part):
    key_inter, key_env, key_out = jax.random.split(key, 3)
    shape = (GROUPS, OWNERS, RIGHT_TASKS)
    columns = [jax.random.randint(key_inter, shape, 0, INTER_TILES), jax.random.randint(key_env, shape, 0, ENV_TILES), jax.random.randint(key_out, shape, 0, TILE_DEV)]
    return jnp.stack(columns, axis=-1).astype(jnp.int32)


def shard_levels(rng, dims, cuts, least, largest):
    loudness, own = 1.0, jax.random.fold_in(rng, 6)
    for position, shards_of in cuts:
        steps = jnp.exp(jax.random.uniform(jax.random.fold_in(own, position), (shards_of,), jnp.float32, least / len(cuts), largest / len(cuts)))
        loudness = loudness * jnp.repeat(steps, dims[position] // shards_of).reshape([-1 if axis == position else 1 for axis in range(len(dims))])
    return loudness


def gaussian(rng, extent, spread, reach, cuts=(), kind=jnp.bfloat16):
    drawn = jax.random.normal(rng, extent, jnp.float32) * spread
    if len(cuts) > 0:
        drawn = shard_levels(rng, extent, cuts, -0.22, 0.18) * drawn
    return jnp.clip(drawn, min=-reach, max=reach).astype(kind)


def setup_inputs(seed: int = 0) -> dict:
    splits = jax.random.split(jax.random.key(seed), 7)
    wave_tiles = gaussian(splits[0], (ALL_TILES, VECTORS, TILE_DIM, TILE_DIM), 1.0, 6.0, ((0, 64),))
    left_env = gaussian(splits[1], (GROUPS, ENV_TILES, TILE_DIM, TILE_DIM), TILE_DIM ** -0.5, 0.5, ((0, 8), (1, 64)))
    right_env = gaussian(splits[2], (GROUPS, ENV_TILES, TILE_DIM, TILE_DIM), TILE_DIM ** -0.5, 0.5, ((0, 8), (1, 64)))
    send_list = draw_send_list(jax.random.fold_in(splits[6], 71), 0)
    left_tasks = draw_left_tasks(jax.random.fold_in(splits[6], 71), 0)
    right_tasks = draw_right_tasks(jax.random.fold_in(splits[6], 71), 0)
    return {"wave_tiles": wave_tiles, "left_env": left_env, "right_env": right_env, "send_list": send_list, "left_tasks": left_tasks, "right_tasks": right_tasks}


def one_group(received, env_left, env_right, left_rows, right_rows):
    left_tiles = jnp.take(env_left, left_rows[:, 0], axis=0).astype(jnp.float32)
    wave_part = jnp.take(received, left_rows[:, 1], axis=0).astype(jnp.float32)
    products = jnp.einsum("bij,bvjk->bvik", left_tiles, wave_part, precision=lax.Precision.HIGHEST)
    inter = jax.ops.segment_sum(products, left_rows[:, 2], num_segments=INTER_TILES).astype(jnp.bfloat16)
    inter_part = jnp.take(inter, right_rows[:, 0], axis=0).astype(jnp.float32)
    right_tiles = jnp.take(env_right, right_rows[:, 1], axis=0).astype(jnp.float32)
    products = jnp.einsum("bvij,bjk->bvik", inter_part, right_tiles, precision=lax.Precision.HIGHEST)
    return jax.ops.segment_sum(products, right_rows[:, 2], num_segments=TILE_DEV)


def reference(wave_tiles, left_env, right_env, send_list, left_tasks, right_tasks):
    by_owner = jnp.transpose(send_list.reshape(OWNERS, OWNERS, CAPACITY), (1, 0, 2))
    left_owner = jnp.swapaxes(left_tasks, 0, 1)
    right_owner = jnp.swapaxes(right_tasks, 0, 1)
    senders = jnp.arange(OWNERS, dtype=jnp.int32)

    def per_owner(inputs):
        local_list, left_rows, right_rows = inputs
        global_index = (senders[:, None] * TILE_DEV + jnp.maximum(local_list, 0)).reshape(-1).astype(jnp.int32)
        live = (local_list >= 0).reshape(-1)
        received = jnp.where(live[:, None, None, None], jnp.take(wave_tiles, global_index, axis=0), jnp.zeros((), jnp.bfloat16))

        def add_group(total, group_inputs):
            env_left, env_right, left_one, right_one = group_inputs
            return total + one_group(received, env_left, env_right, left_one, right_one), None

        start = jnp.zeros((TILE_DEV, VECTORS, TILE_DIM, TILE_DIM), jnp.float32)
        total, unused = lax.scan(add_group, start, (left_env, right_env, left_rows, right_rows))
        return total

    result = lax.map(per_owner, (by_owner, left_owner, right_owner))
    return result.reshape(ALL_TILES, VECTORS, TILE_DIM, TILE_DIM)
```

```python
import functools

import jax
import jax.numpy as jnp
from jax import lax
from jax.experimental import pallas as pl
from jax.experimental.pallas import tpu as pltpu
from jax.sharding import Mesh
from jax.sharding import PartitionSpec as P

INTER_TILES = 32
TILES = 16
LEFT = 96
RIGHT = 256
AXES = ("z", "x", "y", "core")
SWAP = []
for _z in range(8):
    for _x in range(4):
        for _y in range(8):
            for _c in range(2):
                source = ((_z * 4 + _x) * 8 + _y) * 2 + _c
                target = (((2 * _x + _c) * 4 + _z // 2) * 8 + _y) * 2 + _z % 2
                SWAP.append((source, target))


def tasks_kernel(ltask, rtask, wave_ref, left_ref, right_ref, out_ref, acc, inter, total):
    acc[...] = jnp.zeros_like(acc)
    total[...] = jnp.zeros_like(total)

    def left_step(t, carry):
        e, s, x = ltask[3 * t], ltask[3 * t + 1], ltask[3 * t + 2]
        rhs = jnp.concatenate([wave_ref[s, 0], wave_ref[s, 1]], axis=1)
        acc[x] += jnp.dot(left_ref[e], rhs, preferred_element_type=jnp.float32)
        return carry

    lax.fori_loop(0, LEFT, left_step, 0, unroll=4)
    for v in range(2):
        inter[:, v] = acc[:, :, 128 * v : 128 * (v + 1)].astype(jnp.bfloat16)

    def right_step(t, carry):
        x, e, k = rtask[3 * t], rtask[3 * t + 1], rtask[3 * t + 2]
        lhs = inter[x].reshape(256, 128)
        total[k] += jnp.dot(lhs, right_ref[e], preferred_element_type=jnp.float32)
        return carry

    lax.fori_loop(0, RIGHT, right_step, 0, unroll=4)
    for k in range(TILES):
        out_ref[:, k] = jnp.swapaxes(total[k].reshape(2, 8, 16, 128), 0, 1)


def run_tasks(ltask, rtask, wave, left, right):
    vmem = pl.BlockSpec(memory_space=pltpu.VMEM)
    smem = pl.BlockSpec(memory_space=pltpu.SMEM)
    return pl.pallas_call(
        tasks_kernel,
        out_shape=jax.ShapeDtypeStruct((8, TILES, 2, 16, 128), jnp.float32),
        in_specs=[smem, smem, vmem, vmem, vmem],
        out_specs=vmem,
        scratch_shapes=[
            pltpu.VMEM((INTER_TILES, 128, 256), jnp.float32),
            pltpu.VMEM((INTER_TILES, 2, 128, 128), jnp.bfloat16),
            pltpu.VMEM((TILES, 256, 128), jnp.float32),
        ],
        compiler_params=pltpu.CompilerParams(vmem_limit_bytes=44 << 20),
        name="tasks",
    )(ltask, rtask, wave, left, right)


def shards(wave_tiles, left_env, right_env, send_list, left_tasks, right_tasks):
    z = lax.axis_index("z")
    left_rows, right_rows = left_tasks[0, 0], right_tasks[0, 0]
    env_place = lambda e: (((e >> 1) & 7) << 3) | ((e >> 4) << 1) | (e & 1)
    slot = left_rows[:, 1]
    sender = slot >> 1
    place = ((((sender >> 4) << 1) | (sender & 1)) << 4) | (((sender >> 1) & 7) << 1) | (slot & 1)
    left_rows = jnp.stack([env_place(left_rows[:, 0]), place, left_rows[:, 2]], axis=1)
    right_rows = jnp.stack(
        [right_rows[:, 0], env_place(right_rows[:, 1]), right_rows[:, 2]], axis=1
    )
    rows = jnp.concatenate([left_rows, right_rows], axis=0).reshape(-1)
    rows = lax.ppermute(rows, AXES, SWAP)
    ltask, rtask = rows[: 3 * LEFT], rows[3 * LEFT :]

    env = jnp.stack([left_env[0, 0], right_env[0, 0]])
    env = lax.ppermute(env, AXES, SWAP)
    left = lax.all_gather(env[0], ("y", "z"), axis=0)
    right = lax.all_gather(env[1], ("y", "z"), axis=0)

    chosen = lax.dynamic_index_in_dim(send_list.reshape(4, 8, 2, 2), z // 2, 0, False)
    chosen = lax.dynamic_index_in_dim(chosen, z % 2, 1, False).reshape(16)
    picked = jnp.take(wave_tiles, jnp.maximum(chosen, 0), axis=0)
    outgoing = jnp.where((chosen >= 0)[:, None, None, None], picked, jnp.zeros((), jnp.bfloat16))
    arrived = lax.all_to_all(outgoing, "y", split_axis=0, concat_axis=0, tiled=True)
    wave = lax.all_gather(arrived, ("x", "core"), axis=0, tiled=True)

    partial = run_tasks(ltask, rtask, wave, left, right)
    summed = lax.psum_scatter(partial, ("x", "core"), scatter_dimension=0, tiled=False)
    return lax.ppermute(summed, AXES, SWAP)


def solution(mesh):
    fine = Mesh(mesh.devices.reshape(8, 4, 8, 2), AXES)
    sector = ("x", "y", "core")
    in_specs = (
        P(sector, None, None, None),
        P("z", sector, None, None),
        P("z", sector, None, None),
        P(sector, None),
        P("z", sector, None, None),
        P("z", sector, None, None),
    )
    out_specs = P(sector, None, "z", None)
    return jax.shard_map(shards, mesh=fine, in_specs=in_specs, out_specs=out_specs, check_vma=False)
```

```python
import jax
import jax.numpy as jnp
from jax import lax
from jax.experimental import pallas as pl
from jax.experimental.pallas import tpu as pltpu
from jax.sharding import Mesh
from jax.sharding import PartitionSpec as P

INTER_TILES = 32
TILES = 16
LEFT = 96
RIGHT = 256
ROWS = 16
AXES = ("z", "x", "y", "core")
MESH = pl.DeviceIdType.MESH
ANY = pl.BlockSpec(memory_space=pl.ANY)
VMEM = pl.BlockSpec(memory_space=pltpu.VMEM)
SMEM = pl.BlockSpec(memory_space=pltpu.SMEM)


def place():
    return tuple(lax.axis_index(name) for name in AXES)


def swapped(z, x, y, c):
    return (2 * x + c, z // 2, y, z % 2)


def greet(peers, partner, fixed):
    barrier = pltpu.get_barrier_semaphore()
    for peer in peers:
        pl.semaphore_signal(barrier, inc=1, device_id=peer, device_id_type=MESH)

    @pl.when(jnp.logical_not(fixed))
    def _():
        pl.semaphore_signal(barrier, inc=1, device_id=partner, device_id_type=MESH)

    pl.semaphore_wait(barrier, len(peers) + jnp.where(fixed, 0, 1))


def gather_kernel(
    rows_in, left_in, right_in, outgoing, rows, env, wave,
    wrecv, erecv, mate_recv, rows_recv, send,
):
    z, x, y, c = place()
    xc = 2 * x + c
    fixed = z == xc
    partner = swapped(z, x, y, c)
    mate = (z, x, y, 1 - c)
    xup, xdown = (z, (x + 1) % 4, y, c), (z, (x + 3) % 4, y, c)
    zup, zdown = ((z + 1) % 8, x, y, c), ((z + 7) % 8, x, y, c)
    others = [(z, x, (y + d) % 8, c) for d in range(1, 8)]
    greet(others + [mate, xup, xdown, zup, zdown], partner, fixed)
    Y_SEND, EY_SEND, MATE_SEND, XUP, XDOWN, ZUP, ZDOWN, E_SEND, ROWS_SEND = range(9)

    def remote(source, target, sender, receiver, device):
        pltpu.make_async_remote_copy(
            src_ref=source, dst_ref=target, send_sem=send.at[sender], recv_sem=receiver,
            device_id=device, device_id_type=MESH,
        ).start()

    def wait(ref, sem):
        pltpu.make_async_copy(ref, ref, sem).wait()

    def pass_wave(slot, sender, device):
        remote(wave.at[slot], wave.at[slot], sender, wrecv.at[slot], device)

    def pass_mate(slot):
        remote(wave.at[slot], wave.at[slot], MATE_SEND, mate_recv, mate)

    def pass_env(slot, sender, device):
        remote(env.at[slot], env.at[slot], sender, erecv.at[slot], device)

    theirs = xc * 8 + y

    @pl.when(fixed)
    def _():
        pltpu.make_async_copy(left_in, env.at[theirs, 0], erecv.at[theirs]).start()
        pltpu.make_async_copy(right_in, env.at[theirs, 1], erecv.at[theirs]).start()
        pltpu.make_async_copy(rows_in, rows, rows_recv).start()

    @pl.when(jnp.logical_not(fixed))
    def _():
        remote(left_in, env.at[theirs, 0], E_SEND, erecv.at[theirs], partner)
        remote(right_in, env.at[theirs, 1], E_SEND, erecv.at[theirs], partner)
        remote(rows_in, rows, ROWS_SEND, rows_recv, partner)

    mine = xc * 8 + y
    pltpu.make_async_copy(outgoing.at[y], wave.at[mine], wrecv.at[mine]).start()
    for d in (1, 7):
        remote(outgoing.at[(y + d) % 8], wave.at[mine], Y_SEND, wrecv.at[mine], others[d - 1])
    own = z * 8 + y
    wait(env.at[own], erecv.at[own])
    for d in (1, 7, 2, 6, 3, 5, 4):
        pass_env(own, EY_SEND, others[d - 1])
    for d in (2, 6, 3, 5, 4):
        remote(outgoing.at[(y + d) % 8], wave.at[mine], Y_SEND, wrecv.at[mine], others[d - 1])

    def source(r):
        step = (r + 1) // 2
        return (y + jnp.where(r % 2 == 1, step, 8 - step)) % 8

    def turn(i, carry):
        @pl.when(i < 8)
        def _():
            yy = source(i)
            slot = xc * 8 + yy
            wait(wave.at[slot], wrecv.at[slot])
            pass_wave(slot, XUP, xup)
            pass_wave(slot, XDOWN, xdown)
            pass_mate(slot)
            slot = z * 8 + yy

            @pl.when(i > 0)
            def _():
                wait(env.at[slot], erecv.at[slot])

            pass_env(slot, ZUP, zup)
            pass_env(slot, ZDOWN, zdown)

        @pl.when(jnp.logical_and(i >= 1, i < 9))
        def _():
            yy = source(i - 1)
            even = yy % 2 == 0
            low = (2 * ((x + 3) % 4) + c) * 8 + yy
            wait(wave.at[low], wrecv.at[low])

            @pl.when(even)
            def _():
                pass_wave(low, XUP, xup)

            pass_mate(low)
            high = (2 * ((x + 1) % 4) + c) * 8 + yy
            wait(wave.at[high], wrecv.at[high])

            @pl.when(jnp.logical_not(even))
            def _():
                pass_wave(high, XDOWN, xdown)

            pass_mate(high)
            low, high = ((z + 7) % 8) * 8 + yy, ((z + 1) % 8) * 8 + yy
            wait(env.at[low], erecv.at[low])
            pass_env(low, ZUP, zup)
            wait(env.at[high], erecv.at[high])
            pass_env(high, ZDOWN, zdown)

        @pl.when(jnp.logical_and(i >= 2, i < 10))
        def _():
            yy = source(i - 2)
            far = (2 * ((x + 2) % 4) + c) * 8 + yy
            wait(wave.at[far], wrecv.at[far])
            pass_mate(far)
            low, high = ((z + 6) % 8) * 8 + yy, ((z + 2) % 8) * 8 + yy
            wait(env.at[low], erecv.at[low])
            pass_env(low, ZUP, zup)
            wait(env.at[high], erecv.at[high])
            pass_env(high, ZDOWN, zdown)

        @pl.when(jnp.logical_and(i >= 3, i < 11))
        def _():
            yy = source(i - 3)
            even = yy % 2 == 0
            low, high = ((z + 5) % 8) * 8 + yy, ((z + 3) % 8) * 8 + yy
            wait(env.at[low], erecv.at[low])

            @pl.when(even)
            def _():
                pass_env(low, ZUP, zup)

            wait(env.at[high], erecv.at[high])

            @pl.when(jnp.logical_not(even))
            def _():
                pass_env(high, ZDOWN, zdown)

        @pl.when(i >= 4)
        def _():
            far = ((z + 4) % 8) * 8 + source(i - 4)
            wait(env.at[far], erecv.at[far])

        return carry

    lax.fori_loop(0, 12, turn, 0)
    wait(rows, rows_recv)
    wait(wave.at[pl.ds(0, 32)], mate_recv)
    wait(wave.at[pl.ds(0, 7)], send.at[Y_SEND])
    wait(env.at[pl.ds(0, 7)], send.at[EY_SEND])
    wait(wave.at[pl.ds(0, 32)], send.at[MATE_SEND])
    wait(wave.at[pl.ds(0, 12)], send.at[XUP])
    wait(wave.at[pl.ds(0, 12)], send.at[XDOWN])
    wait(env.at[pl.ds(0, 28)], send.at[ZUP])
    wait(env.at[pl.ds(0, 28)], send.at[ZDOWN])

    @pl.when(jnp.logical_not(fixed))
    def _():
        wait(env.at[0], send.at[E_SEND])
        wait(rows, send.at[ROWS_SEND])


def gather(rows, left, right, outgoing):
    return pl.pallas_call(
        gather_kernel,
        out_shape=(
            jax.ShapeDtypeStruct((ROWS, 128), jnp.int32),
            jax.ShapeDtypeStruct((64, 2, 128, 128), jnp.bfloat16),
            jax.ShapeDtypeStruct((64, 4, 128, 128), jnp.bfloat16),
        ),
        in_specs=[ANY] * 4,
        out_specs=[ANY] * 3,
        scratch_shapes=[
            pltpu.SemaphoreType.DMA((64,)),
            pltpu.SemaphoreType.DMA((64,)),
            pltpu.SemaphoreType.DMA,
            pltpu.SemaphoreType.DMA,
            pltpu.SemaphoreType.DMA((9,)),
        ],
        compiler_params=pltpu.CompilerParams(collective_id=0, has_side_effects=True),
        name="gather",
    )(rows, left, right, outgoing)


def tasks_kernel(rows, env_any, wave_any, out_ref, env, wave, acc, inter, total, sems):
    loads = [
        pltpu.make_async_copy(wave_any, wave, sems.at[0]),
        pltpu.make_async_copy(env_any, env, sems.at[1]),
    ]
    for load in loads:
        load.start()
    acc[...] = jnp.zeros_like(acc)
    total[...] = jnp.zeros_like(total)
    for load in loads:
        load.wait()

    def left_step(t, carry):
        e, s, x = rows[3 * t], rows[3 * t + 1], rows[3 * t + 2]
        rhs = jnp.concatenate([wave[2 * s], wave[2 * s + 1]], axis=1)
        acc[x] += jnp.dot(env[e, 0], rhs, preferred_element_type=jnp.float32)
        return carry

    lax.fori_loop(0, LEFT, left_step, 0, unroll=4)
    for v in range(2):
        inter[:, v] = acc[:, :, 128 * v : 128 * (v + 1)].astype(jnp.bfloat16)

    def right_step(t, carry):
        base = 3 * (LEFT + t)
        x, e, k = rows[base], rows[base + 1], rows[base + 2]
        lhs = inter[x].reshape(256, 128)
        total[k] += jnp.dot(lhs, env[e, 1], preferred_element_type=jnp.float32)
        return carry

    lax.fori_loop(0, RIGHT, right_step, 0, unroll=4)
    for k in range(TILES):
        out_ref[:, k] = jnp.swapaxes(total[k].reshape(2, 8, 16, 128), 0, 1).astype(jnp.bfloat16)


def run_tasks(rows, env, wave):
    return pl.pallas_call(
        tasks_kernel,
        out_shape=jax.ShapeDtypeStruct((8, TILES, 2, 16, 128), jnp.bfloat16),
        in_specs=[SMEM, ANY, ANY],
        out_specs=VMEM,
        scratch_shapes=[
            pltpu.VMEM((64, 2, 128, 128), jnp.bfloat16),
            pltpu.VMEM((256, 128, 128), jnp.bfloat16),
            pltpu.VMEM((INTER_TILES, 128, 256), jnp.float32),
            pltpu.VMEM((INTER_TILES, 2, 128, 128), jnp.bfloat16),
            pltpu.VMEM((TILES, 256, 128), jnp.float32),
            pltpu.SemaphoreType.DMA((2,)),
        ],
        compiler_params=pltpu.CompilerParams(vmem_limit_bytes=44 << 20),
        name="tasks",
    )(rows, env, wave)


def reduce_kernel(partial, out, parts, result, arrived, recv, send, last_recv, last_send):
    z, x, y, c = place()
    xc = 2 * x + c
    fixed = z == xc
    partner = swapped(z, x, y, c)
    peers = []
    for k in range(1, 8):
        to = (xc + k) % 8
        peers.append((z, to // 2, y, to % 2))
    greet(peers, partner, fixed)
    copies = []
    for k in (1, 7, 2, 6, 3, 5, 4):
        copy = pltpu.make_async_remote_copy(
            src_ref=partial.at[(xc + k) % 8], dst_ref=parts.at[k],
            send_sem=send.at[k], recv_sem=recv.at[k],
            device_id=peers[k - 1], device_id_type=MESH,
        )
        copy.start()
        copies.append(copy)
    for copy in copies:
        copy.wait_recv()
    for h in range(2):
        rows = pl.ds(256 * h, 256)
        total = partial[xc, rows].astype(jnp.float32)
        for k in range(1, 8):
            total += parts[k, rows].astype(jnp.float32)
        result[rows] = total.astype(jnp.bfloat16)

        @pl.when(fixed)
        def _():
            pltpu.make_async_copy(result.at[rows], arrived.at[rows], last_recv.at[h]).start()

        @pl.when(jnp.logical_not(fixed))
        def _():
            pltpu.make_async_remote_copy(
                src_ref=result.at[rows], dst_ref=arrived.at[rows],
                send_sem=last_send.at[h], recv_sem=last_recv.at[h],
                device_id=partner, device_id_type=MESH,
            ).start()

    for copy in copies:
        copy.wait_send()
    for h in range(2):
        rows = pl.ds(256 * h, 256)
        pltpu.make_async_copy(result.at[rows], arrived.at[rows], last_recv.at[h]).wait()
        out[rows] = arrived[rows].astype(jnp.float32)

        @pl.when(jnp.logical_not(fixed))
        def _():
            pltpu.make_async_copy(result.at[rows], arrived.at[rows], last_send.at[h]).wait()


def reduce(partial):
    return pl.pallas_call(
        reduce_kernel,
        out_shape=jax.ShapeDtypeStruct((512, 128), jnp.float32),
        in_specs=[VMEM],
        out_specs=VMEM,
        scratch_shapes=[
            pltpu.VMEM((8, 512, 128), jnp.bfloat16),
            pltpu.VMEM((512, 128), jnp.bfloat16),
            pltpu.VMEM((512, 128), jnp.bfloat16),
            pltpu.SemaphoreType.DMA((8,)),
            pltpu.SemaphoreType.DMA((8,)),
            pltpu.SemaphoreType.DMA((2,)),
            pltpu.SemaphoreType.DMA((2,)),
        ],
        compiler_params=pltpu.CompilerParams(collective_id=1, has_side_effects=True),
        name="reduce",
    )(partial)


def shards(wave_tiles, left_env, right_env, send_list, left_tasks, right_tasks):
    z = lax.axis_index("z")
    left_rows, right_rows = left_tasks[0, 0], right_tasks[0, 0]
    env_place = lambda e: ((e >> 4) << 4) | ((e & 1) << 3) | ((e >> 1) & 7)
    slot = left_rows[:, 1]
    sender = slot >> 1
    spot = ((((sender >> 4) << 1) | (sender & 1)) << 4) | (((sender >> 1) & 7) << 1) | (slot & 1)
    left_rows = jnp.stack([env_place(left_rows[:, 0]), spot, left_rows[:, 2]], axis=1)
    right_rows = jnp.stack(
        [right_rows[:, 0], env_place(right_rows[:, 1]), right_rows[:, 2]], axis=1
    )
    rows = jnp.concatenate([left_rows, right_rows], axis=0).reshape(-1)
    rows = jnp.pad(rows, (0, ROWS * 128 - rows.shape[0])).reshape(ROWS, 128)

    chosen = lax.dynamic_index_in_dim(send_list.reshape(4, 8, 2, 2), z // 2, 0, False)
    chosen = lax.dynamic_index_in_dim(chosen, z % 2, 1, False).reshape(16)
    picked = jnp.take(wave_tiles, jnp.maximum(chosen, 0), axis=0)
    outgoing = jnp.where((chosen >= 0)[:, None, None, None], picked, jnp.zeros((), jnp.bfloat16))

    rows, env, wave = gather(rows, left_env[0, 0], right_env[0, 0], outgoing.reshape(8, 4, 128, 128))
    partial = run_tasks(rows.reshape(-1), env, wave.reshape(256, 128, 128))
    return reduce(partial.reshape(8, 512, 128)).reshape(TILES, 2, 16, 128)


def solution(mesh):
    fine = Mesh(mesh.devices.reshape(8, 4, 8, 2), AXES)
    sector = ("x", "y", "core")
    in_specs = (
        P(sector, None, None, None),
        P("z", sector, None, None),
        P("z", sector, None, None),
        P(sector, None),
        P("z", sector, None, None),
        P("z", sector, None, None),
    )
    out_specs = P(sector, None, "z", None)
    return jax.shard_map(shards, mesh=fine, in_specs=in_specs, out_specs=out_specs, check_vma=False)
```

```python
import jax
import jax.numpy as jnp
from jax import lax
from jax.experimental import pallas as pl
from jax.experimental.pallas import tpu as pltpu
from jax.sharding import Mesh
from jax.sharding import PartitionSpec as P

TILES = 16
LEFT_PAIRS = 64
RIGHT_PAIRS = 136
AXES = ("z", "x", "y", "core")
MESH = pl.DeviceIdType.MESH
ANY = pl.BlockSpec(memory_space=pl.ANY)
VMEM = pl.BlockSpec(memory_space=pltpu.VMEM)
SMEM = pl.BlockSpec(memory_space=pltpu.SMEM)


def place():
    return tuple(lax.axis_index(name) for name in AXES)


def swapped(z, x, y, c):
    return (2 * x + c, z // 2, y, z % 2)


def prep_kernel(wave, picks, left, right, outgoing, lists):
    z = lax.axis_index("z")
    for to in range(8):
        owner = (z // 2 * 8 + to) * 2 + z % 2
        for slot in range(2):
            index = picks[0, 2 * owner + slot]
            tile = wave[jnp.maximum(index, 0)]
            outgoing[2 * to + slot] = jnp.where(index >= 0, tile, jnp.zeros_like(tile))

    def iota(shape, axis):
        return lax.broadcasted_iota(jnp.int32, shape, axis)

    def total(mask, value, axis):
        return jnp.sum(jnp.where(mask, value, 0), axis=axis, keepdims=True)

    def column(row):
        n = row.shape[1]
        return total(iota((n, n), 0) == iota((n, n), 1), row, 1)

    def ordered(row):
        n = row.shape[1]
        down, across = iota((n, n), 0), iota((n, n), 1)
        key = column(row)
        same = key == row
        within = total(jnp.logical_and(same, across < down), 1, 1)
        later = total(jnp.logical_and(same, across > down), 1, 1)
        within_row = total(jnp.logical_and(same, down < across), 1, 0)
        start = total(row < key, 1 - (within_row & 1), 1)
        return key, within, 2 * start + within, later == 0

    def env_place(e):
        return ((e >> 4) << 4) | ((e & 1) << 3) | ((e >> 1) & 7)

    key, within, spot, last = ordered(left[2:3])
    slot = left[1:2]
    sender = slot >> 1
    source = ((((sender >> 4) << 1) | (sender & 1)) << 4) | (((sender >> 1) & 7) << 1) | (slot & 1)
    value = column(env_place(left[0:1]) * 256 + source) + jnp.where(within > 0, 65536, 0)
    n = left.shape[1]
    lists[0:1] = 128 + total(spot == iota((n, 128), 1), value - 128, 0)
    n_right = right.shape[1]
    hit = jnp.logical_and(key == right[0:1], last)
    made = LEFT_PAIRS + total(hit, (spot >> 1) - LEFT_PAIRS, 0)
    key, within, spot, last = ordered(right[2:3])
    value = column(made * 256 + env_place(right[1:2])) + jnp.where(within > 0, 65536, 0)
    empty = LEFT_PAIRS * 256
    for part in range(3):
        place = iota((n_right, 128), 1) + 128 * part
        lists[1 + part : 2 + part] = empty + total(spot == place, value - empty, 0)
    hit = jnp.logical_and(key == iota((n_right, 128), 1), last)
    lists[4:5] = RIGHT_PAIRS + total(hit, (spot >> 1) - RIGHT_PAIRS, 0)
    lists[5:8] = jnp.zeros((3, 128), jnp.int32)


def prep(wave, picks, left, right):
    return pl.pallas_call(
        prep_kernel,
        out_shape=(
            jax.ShapeDtypeStruct((16, 2, 128, 128), jnp.bfloat16),
            jax.ShapeDtypeStruct((8, 128), jnp.int32),
        ),
        in_specs=[VMEM, SMEM, VMEM, VMEM],
        out_specs=(VMEM, VMEM),
        name="prep",
    )(wave, picks, left, right)


def main_kernel(
    lists_in, left_in, right_in, outgoing, out,
    lists_vmem, lists, wave, env, inter, cumulated, partial, parts, result,
    wrecv, erecv, mate_recv, lists_recv, send, recv, part_send, last_recv, last_send,
):
    z, x, y, c = place()
    xc = 2 * x + c
    fixed = z == xc
    partner = swapped(z, x, y, c)
    mate = (z, x, y, 1 - c)
    xup, xdown = (z, (x + 1) % 4, y, c), (z, (x + 3) % 4, y, c)
    zup, zdown = ((z + 1) % 8, x, y, c), ((z + 7) % 8, x, y, c)
    peers = [(z, (xc + k) % 8 // 2, y, (xc + k) % 8 % 2) for k in range(1, 8)]

    barrier = pltpu.get_barrier_semaphore()
    for peer in peers + [zup, zdown] + [(z, x, (y + d) % 8, c) for d in range(1, 8)]:
        pl.semaphore_signal(barrier, inc=1, device_id=peer, device_id_type=MESH)

    @pl.when(jnp.logical_not(fixed))
    def _():
        pl.semaphore_signal(barrier, inc=1, device_id=partner, device_id_type=MESH)

    wave[128] = jnp.zeros((2, 128, 128), jnp.bfloat16)
    inter[LEFT_PAIRS] = jnp.zeros((2, 128, 128), jnp.bfloat16)
    cumulated[RIGHT_PAIRS] = jnp.zeros((256, 128), jnp.bfloat16)
    pl.semaphore_wait(barrier, 16 + jnp.where(fixed, 0, 1))
    Y_SEND, EY_SEND, MATE_SEND, XUP, XDOWN, ZUP, ZDOWN, E_SEND, LISTS_SEND = range(9)

    def remote(source, target, sender, receiver, device):
        pltpu.make_async_remote_copy(
            src_ref=source, dst_ref=target, send_sem=send.at[sender], recv_sem=receiver,
            device_id=device, device_id_type=MESH,
        ).start()

    def wait(ref, sem):
        pltpu.make_async_copy(ref, ref, sem).wait()

    def chunks(slot, count=1):
        return wave.at[pl.ds(2 * slot, 2 * count)]

    def pass_wave(slot, sender, device):
        remote(chunks(slot), chunks(slot), sender, wrecv.at[slot], device)

    def pass_mate(slot):
        remote(chunks(slot), chunks(slot), MATE_SEND, mate_recv, mate)

    def pass_env(slot, sender, device):
        remote(env.at[slot], env.at[slot], sender, erecv.at[slot], device)

    mine = xc * 8 + y

    @pl.when(fixed)
    def _():
        pltpu.make_async_copy(left_in, env.at[mine, 0], erecv.at[mine]).start()
        pltpu.make_async_copy(right_in, env.at[mine, 1], erecv.at[mine]).start()
        pltpu.make_async_copy(lists_in, lists_vmem, lists_recv).start()

    @pl.when(jnp.logical_not(fixed))
    def _():
        remote(left_in, env.at[mine, 0], E_SEND, erecv.at[mine], partner)
        remote(right_in, env.at[mine, 1], E_SEND, erecv.at[mine], partner)
        remote(lists_in, lists_vmem, LISTS_SEND, lists_recv, partner)

    own = z * 8 + y

    def shift(r):
        step = (r + 1) // 2
        return jnp.where(r % 2 == 1, step, 8 - step)

    def send_wave(r):
        to = (y + 8 - shift(r)) % 8
        remote(outgoing.at[pl.ds(2 * to, 2)], chunks(mine), Y_SEND, wrecv.at[mine], (z, x, to, c))

    def send_env(r):
        to = (y + 8 - shift(r)) % 8
        remote(env.at[own], env.at[own], EY_SEND, erecv.at[own], (z, x, to, c))

    here = outgoing.at[pl.ds(2 * y, 2)]
    pltpu.make_async_copy(here, chunks(mine), wrecv.at[mine]).start()
    for r in range(1, 5):
        send_wave(r)
    remote(here, chunks(mine), XUP, wrecv.at[mine], xup)
    remote(here, chunks(mine), XDOWN, wrecv.at[mine], xdown)
    remote(here, chunks(mine), MATE_SEND, mate_recv, mate)
    wait(env.at[own], erecv.at[own])
    for r in range(1, 5):
        send_env(r)

    def source(r):
        return (y + shift(r)) % 8

    def turn(i, carry):
        @pl.when(i < 3)
        def _():
            send_env(i + 5)
            send_wave(i + 5)

        @pl.when(i < 8)
        def _():
            yy = source(i)
            slot = xc * 8 + yy

            @pl.when(i > 0)
            def _():
                wait(chunks(slot), wrecv.at[slot])
                pass_wave(slot, XUP, xup)
                pass_wave(slot, XDOWN, xdown)
                pass_mate(slot)

            slot = z * 8 + yy

            @pl.when(i > 0)
            def _():
                wait(env.at[slot], erecv.at[slot])

            pass_env(slot, ZUP, zup)
            pass_env(slot, ZDOWN, zdown)

        @pl.when(jnp.logical_and(i >= 1, i < 9))
        def _():
            yy = source(i - 1)
            even = yy % 2 == 0
            low = (2 * ((x + 3) % 4) + c) * 8 + yy
            wait(chunks(low), wrecv.at[low])

            @pl.when(even)
            def _():
                pass_wave(low, XUP, xup)

            pass_mate(low)
            high = (2 * ((x + 1) % 4) + c) * 8 + yy
            wait(chunks(high), wrecv.at[high])

            @pl.when(jnp.logical_not(even))
            def _():
                pass_wave(high, XDOWN, xdown)

            pass_mate(high)
            low, high = ((z + 7) % 8) * 8 + yy, ((z + 1) % 8) * 8 + yy
            wait(env.at[low], erecv.at[low])
            pass_env(low, ZUP, zup)
            wait(env.at[high], erecv.at[high])
            pass_env(high, ZDOWN, zdown)

        @pl.when(jnp.logical_and(i >= 2, i < 10))
        def _():
            yy = source(i - 2)
            far = (2 * ((x + 2) % 4) + c) * 8 + yy
            wait(chunks(far), wrecv.at[far])
            pass_mate(far)
            low, high = ((z + 6) % 8) * 8 + yy, ((z + 2) % 8) * 8 + yy
            wait(env.at[low], erecv.at[low])
            pass_env(low, ZUP, zup)
            wait(env.at[high], erecv.at[high])
            pass_env(high, ZDOWN, zdown)

        @pl.when(jnp.logical_and(i >= 3, i < 11))
        def _():
            yy = source(i - 3)
            even = yy % 2 == 0
            low, high = ((z + 5) % 8) * 8 + yy, ((z + 3) % 8) * 8 + yy
            wait(env.at[low], erecv.at[low])

            @pl.when(even)
            def _():
                pass_env(low, ZUP, zup)

            wait(env.at[high], erecv.at[high])

            @pl.when(jnp.logical_not(even))
            def _():
                pass_env(high, ZDOWN, zdown)

        @pl.when(i >= 4)
        def _():
            far = ((z + 4) % 8) * 8 + source(i - 4)
            wait(env.at[far], erecv.at[far])

        return carry

    lax.fori_loop(0, 12, turn, 0)

    wait(lists_vmem, lists_recv)
    load = pltpu.make_async_copy(lists_vmem, lists, lists_recv)
    load.start()
    wait(chunks(mine), wrecv.at[mine])
    wait(chunks(0, 32), mate_recv)
    load.wait()

    def left_pair(p, total):
        one, two = lists[0, 2 * p], lists[0, 2 * p + 1]
        lhs = jnp.concatenate([env[(one >> 8) & 63, 0], env[(two >> 8) & 63, 0]], axis=1)
        rhs = jnp.concatenate(
            [
                jnp.concatenate([wave[one & 255, 0], wave[one & 255, 1]], axis=1),
                jnp.concatenate([wave[two & 255, 0], wave[two & 255, 1]], axis=1),
            ],
            axis=0,
        )
        product = jnp.dot(lhs, rhs, preferred_element_type=jnp.float32)
        total = product + total * (one >> 16).astype(jnp.float32)
        inter[p, 0] = total[:, :128].astype(jnp.bfloat16)
        inter[p, 1] = total[:, 128:].astype(jnp.bfloat16)
        return total

    lax.fori_loop(0, LEFT_PAIRS, left_pair, jnp.zeros((128, 256), jnp.float32), unroll=8)

    def right_pair(p, total):
        row, column = 1 + p // 64, 2 * (p % 64)
        one, two = lists[row, column], lists[row, column + 1]
        lhs = jnp.concatenate(
            [
                inter[(one >> 8) & 127].reshape(256, 128),
                inter[(two >> 8) & 127].reshape(256, 128),
            ],
            axis=1,
        )
        rhs = jnp.concatenate([env[one & 63, 1], env[two & 63, 1]], axis=0)
        product = jnp.dot(lhs, rhs, preferred_element_type=jnp.float32)
        total = product + total * (one >> 16).astype(jnp.float32)
        cumulated[p] = total.astype(jnp.bfloat16)
        return total

    lax.fori_loop(0, RIGHT_PAIRS, right_pair, jnp.zeros((256, 128), jnp.float32), unroll=8)
    for k in range(TILES):
        tile = cumulated[lists[4, k]].reshape(2, 8, 16, 128)
        partial[:, k] = jnp.swapaxes(tile, 0, 1)

    def part(k):
        return pltpu.make_async_remote_copy(
            src_ref=partial.at[(xc + k) % 8], dst_ref=parts.at[k],
            send_sem=part_send.at[k], recv_sem=recv.at[k],
            device_id=peers[k - 1], device_id_type=MESH,
        )

    copies = [part(k) for k in (1, 7, 2, 6, 3, 5, 4)]
    for copy in copies:
        copy.start()
    for copy in copies:
        copy.wait_recv()
    for h in range(2):
        half = pl.ds(8 * h, 8)
        total = partial[xc, half].astype(jnp.float32)
        for k in range(1, 8):
            total += parts[k, half].astype(jnp.float32)
        result[half] = total.astype(jnp.bfloat16)

        @pl.when(fixed)
        def _():
            pltpu.make_async_copy(result.at[half], out.at[half], last_recv.at[h]).start()

        @pl.when(jnp.logical_not(fixed))
        def _():
            pltpu.make_async_remote_copy(
                src_ref=result.at[half], dst_ref=out.at[half],
                send_sem=last_send.at[h], recv_sem=last_recv.at[h],
                device_id=partner, device_id_type=MESH,
            ).start()

    wait(chunks(0, 7), send.at[Y_SEND])
    wait(env.at[pl.ds(0, 7)], send.at[EY_SEND])
    wait(chunks(0, 32), send.at[MATE_SEND])
    wait(chunks(0, 12), send.at[XUP])
    wait(chunks(0, 12), send.at[XDOWN])
    wait(env.at[pl.ds(0, 28)], send.at[ZUP])
    wait(env.at[pl.ds(0, 28)], send.at[ZDOWN])
    for copy in copies:
        copy.wait_send()

    @pl.when(jnp.logical_not(fixed))
    def _():
        wait(env.at[0], send.at[E_SEND])
        wait(lists_vmem, send.at[LISTS_SEND])
        for h in range(2):
            wait(result.at[pl.ds(8 * h, 8)], last_send.at[h])

    for h in range(2):
        wait(result.at[pl.ds(8 * h, 8)], last_recv.at[h])


def main(lists, left, right, outgoing):
    return pl.pallas_call(
        main_kernel,
        out_shape=jax.ShapeDtypeStruct((TILES, 2, 16, 128), jnp.bfloat16),
        in_specs=[VMEM, ANY, ANY, VMEM],
        out_specs=VMEM,
        scratch_shapes=[
            pltpu.VMEM((8, 128), jnp.int32),
            pltpu.SMEM((8, 128), jnp.int32),
            pltpu.VMEM((129, 2, 128, 128), jnp.bfloat16),
            pltpu.VMEM((64, 2, 128, 128), jnp.bfloat16),
            pltpu.VMEM((LEFT_PAIRS + 1, 2, 128, 128), jnp.bfloat16),
            pltpu.VMEM((RIGHT_PAIRS + 1, 256, 128), jnp.bfloat16),
            pltpu.VMEM((8, TILES, 2, 16, 128), jnp.bfloat16),
            pltpu.VMEM((8, TILES, 2, 16, 128), jnp.bfloat16),
            pltpu.VMEM((TILES, 2, 16, 128), jnp.bfloat16),
            pltpu.SemaphoreType.DMA((64,)),
            pltpu.SemaphoreType.DMA((64,)),
            pltpu.SemaphoreType.DMA,
            pltpu.SemaphoreType.DMA,
            pltpu.SemaphoreType.DMA((9,)),
            pltpu.SemaphoreType.DMA((8,)),
            pltpu.SemaphoreType.DMA((8,)),
            pltpu.SemaphoreType.DMA((2,)),
            pltpu.SemaphoreType.DMA((2,)),
        ],
        compiler_params=pltpu.CompilerParams(
            collective_id=0, has_side_effects=True, vmem_limit_bytes=44 << 20
        ),
        name="main",
    )(lists, left, right, outgoing)


def shards(wave_tiles, left_env, right_env, send_list, left_tasks, right_tasks):
    outgoing, lists = prep(wave_tiles, send_list, left_tasks[0, 0].T, right_tasks[0, 0].T)
    rows = main(lists, left_env[0, 0], right_env[0, 0], outgoing)
    return rows.astype(jnp.float32)


def solution(mesh):
    fine = Mesh(mesh.devices.reshape(8, 4, 8, 2), AXES)
    sector = ("x", "y", "core")
    in_specs = (
        P(sector, None, None, None),
        P("z", sector, None, None),
        P("z", sector, None, None),
        P(sector, None),
        P("z", sector, None, None),
        P("z", sector, None, None),
    )
    out_specs = P(sector, None, "z", None)
    return jax.shard_map(shards, mesh=fine, in_specs=in_specs, out_specs=out_specs, check_vma=False)
```

```python
import jax
import jax.numpy as jnp
from jax import lax
from jax.experimental import pallas as pl
from jax.experimental.pallas import tpu as pltpu
from jax.sharding import Mesh
from jax.sharding import PartitionSpec as P

TILES = 16
LEFT_PAIRS = 64
RIGHT_PAIRS = 136
STEPS = 4
AXES = ("z", "x", "y", "core")
MESH = pl.DeviceIdType.MESH
ANY = pl.BlockSpec(memory_space=pl.ANY)
VMEM = pl.BlockSpec(memory_space=pltpu.VMEM)
SMEM = pl.BlockSpec(memory_space=pltpu.SMEM)


def place():
    return tuple(lax.axis_index(name) for name in AXES)


def swapped(z, x, y, c):
    return (2 * x + c, z // 2, y, z % 2)


def build_lists(left, right, lists):
    def iota(shape, axis):
        return lax.broadcasted_iota(jnp.int32, shape, axis)

    def total(mask, value, axis):
        return jnp.sum(jnp.where(mask, value, 0), axis=axis, keepdims=True)

    def column(row):
        n = row.shape[1]
        return total(iota((n, n), 0) == iota((n, n), 1), row, 1)

    def ordered(row):
        n = row.shape[1]
        down, across = iota((n, n), 0), iota((n, n), 1)
        key = column(row)
        same = key == row
        within = total(jnp.logical_and(same, across < down), 1, 1)
        later = total(jnp.logical_and(same, across > down), 1, 1)
        within_row = total(jnp.logical_and(same, down < across), 1, 0)
        start = total(row < key, 1 - (within_row & 1), 1)
        return key, within, 2 * start + within, later == 0

    def env_place(e):
        return ((e >> 4) << 4) | ((e & 1) << 3) | ((e >> 1) & 7)

    key, within, spot, last = ordered(left[2])
    slot = left[1]
    sender = slot >> 1
    source = ((((sender >> 4) << 1) | (sender & 1)) << 4) | (((sender >> 1) & 7) << 1) | (slot & 1)
    value = column(env_place(left[0]) * 256 + source) + jnp.where(within > 0, 65536, 0)
    n = left.shape[2]
    lists[0:1] = 128 + total(spot == iota((n, 128), 1), value - 128, 0)
    n_right = right.shape[2]
    hit = jnp.logical_and(key == right[0], last)
    made = LEFT_PAIRS + total(hit, (spot >> 1) - LEFT_PAIRS, 0)
    key, within, spot, last = ordered(right[2])
    value = column(made * 256 + env_place(right[1])) + jnp.where(within > 0, 65536, 0)
    empty = LEFT_PAIRS * 256
    for part in range(3):
        place = iota((n_right, 128), 1) + 128 * part
        lists[1 + part : 2 + part] = empty + total(spot == place, value - empty, 0)
    hit = jnp.logical_and(key == iota((n_right, 128), 1), last)
    lists[4:5] = RIGHT_PAIRS + total(hit, (spot >> 1) - RIGHT_PAIRS, 0)
    lists[5:8] = jnp.zeros((3, 128), jnp.int32)


def main_kernel(
    wave_in, picks, left_in, right_in, left_tasks, right_tasks, out,
    tiles, outgoing, lists_in, lists_vmem, lists, wave, env, inter, cumulated, partial, parts, result,
    wrecv, erecv, mate_recv, lists_recv, send, recv, part_send, last_recv, last_send, tiles_recv,
):
    z, x, y, c = place()
    xc = 2 * x + c
    fixed = z == xc
    partner = swapped(z, x, y, c)
    mate = (z, x, y, 1 - c)
    xup, xdown = (z, (x + 1) % 4, y, c), (z, (x + 3) % 4, y, c)
    zup, zdown = ((z + 1) % 8, x, y, c), ((z + 7) % 8, x, y, c)
    peers = [(z, (xc + k) % 8 // 2, y, (xc + k) % 8 % 2) for k in range(1, 8)]

    fetch = pltpu.make_async_copy(wave_in, tiles, tiles_recv)
    fetch.start()
    barrier = pltpu.get_barrier_semaphore()
    for peer in peers + [zup, zdown] + [(z, x, (y + d) % 8, c) for d in range(1, 8)]:
        pl.semaphore_signal(barrier, inc=1, device_id=peer, device_id_type=MESH)

    @pl.when(jnp.logical_not(fixed))
    def _():
        pl.semaphore_signal(barrier, inc=1, device_id=partner, device_id_type=MESH)

    wave[128] = jnp.zeros((2, 128, 128), jnp.bfloat16)
    inter[LEFT_PAIRS] = jnp.zeros((2, 128, 128), jnp.bfloat16)
    cumulated[RIGHT_PAIRS] = jnp.zeros((256, 128), jnp.bfloat16)
    fetch.wait()
    for to in range(8):
        owner = (z // 2 * 8 + to) * 2 + z % 2
        for slot in range(2):
            index = picks[0, 2 * owner + slot]
            tile = tiles[jnp.maximum(index, 0)]
            outgoing[2 * to + slot] = jnp.where(index >= 0, tile, jnp.zeros_like(tile))

    pl.semaphore_wait(barrier, 16 + jnp.where(fixed, 0, 1))
    Y_SEND, EY_SEND, MATE_SEND, XUP, XDOWN, ZUP, ZDOWN, E_SEND, LISTS_SEND = range(9)

    def remote(source, target, sender, receiver, device):
        pltpu.make_async_remote_copy(
            src_ref=source, dst_ref=target, send_sem=send.at[sender], recv_sem=receiver,
            device_id=device, device_id_type=MESH,
        ).start()

    def wait(ref, sem):
        pltpu.make_async_copy(ref, ref, sem).wait()

    def chunks(slot, count=1):
        return wave.at[pl.ds(2 * slot, 2 * count)]

    def pass_wave(slot, sender, device):
        remote(chunks(slot), chunks(slot), sender, wrecv.at[slot], device)

    def pass_mate(slot):
        remote(chunks(slot), chunks(slot), MATE_SEND, mate_recv, mate)

    def pass_env(slot, sender, device):
        remote(env.at[slot], env.at[slot], sender, erecv.at[slot], device)

    mine = xc * 8 + y

    @pl.when(fixed)
    def _():
        pltpu.make_async_copy(left_in, env.at[mine, 0], erecv.at[mine]).start()
        pltpu.make_async_copy(right_in, env.at[mine, 1], erecv.at[mine]).start()

    @pl.when(jnp.logical_not(fixed))
    def _():
        remote(left_in, env.at[mine, 0], E_SEND, erecv.at[mine], partner)
        remote(right_in, env.at[mine, 1], E_SEND, erecv.at[mine], partner)

    own = z * 8 + y

    def shift(r):
        step = (r + 1) // 2
        return jnp.where(r % 2 == 1, step, 8 - step)

    def send_wave(r):
        to = (y + 8 - shift(r)) % 8
        remote(outgoing.at[pl.ds(2 * to, 2)], chunks(mine), Y_SEND, wrecv.at[mine], (z, x, to, c))

    def send_env(r):
        to = (y + 8 - shift(r)) % 8
        remote(env.at[own], env.at[own], EY_SEND, erecv.at[own], (z, x, to, c))

    here = outgoing.at[pl.ds(2 * y, 2)]
    pltpu.make_async_copy(here, chunks(mine), wrecv.at[mine]).start()
    for r in range(1, 5):
        send_wave(r)
    remote(here, chunks(mine), XUP, wrecv.at[mine], xup)
    remote(here, chunks(mine), XDOWN, wrecv.at[mine], xdown)
    remote(here, chunks(mine), MATE_SEND, mate_recv, mate)
    build_lists(left_tasks, right_tasks, lists_in)

    @pl.when(fixed)
    def _():
        pltpu.make_async_copy(lists_in, lists_vmem, lists_recv).start()

    @pl.when(jnp.logical_not(fixed))
    def _():
        remote(lists_in, lists_vmem, LISTS_SEND, lists_recv, partner)

    wait(env.at[own], erecv.at[own])
    for r in range(1, 5):
        send_env(r)

    def source(r):
        return (y + shift(r)) % 8

    def turn(i, carry):
        @pl.when(i < 3)
        def _():
            send_env(i + 5)
            send_wave(i + 5)

        @pl.when(i < 8)
        def _():
            yy = source(i)
            slot = xc * 8 + yy

            @pl.when(i > 0)
            def _():
                wait(chunks(slot), wrecv.at[slot])
                pass_wave(slot, XUP, xup)
                pass_wave(slot, XDOWN, xdown)
                pass_mate(slot)

            slot = z * 8 + yy

            @pl.when(i > 0)
            def _():
                wait(env.at[slot], erecv.at[slot])

            pass_env(slot, ZUP, zup)
            pass_env(slot, ZDOWN, zdown)

        @pl.when(jnp.logical_and(i >= 1, i < 9))
        def _():
            yy = source(i - 1)
            even = yy % 2 == 0
            low = (2 * ((x + 3) % 4) + c) * 8 + yy
            wait(chunks(low), wrecv.at[low])

            @pl.when(even)
            def _():
                pass_wave(low, XUP, xup)

            pass_mate(low)
            high = (2 * ((x + 1) % 4) + c) * 8 + yy
            wait(chunks(high), wrecv.at[high])

            @pl.when(jnp.logical_not(even))
            def _():
                pass_wave(high, XDOWN, xdown)

            pass_mate(high)
            low, high = ((z + 7) % 8) * 8 + yy, ((z + 1) % 8) * 8 + yy
            wait(env.at[low], erecv.at[low])
            pass_env(low, ZUP, zup)
            wait(env.at[high], erecv.at[high])
            pass_env(high, ZDOWN, zdown)

        @pl.when(jnp.logical_and(i >= 2, i < 10))
        def _():
            yy = source(i - 2)
            far = (2 * ((x + 2) % 4) + c) * 8 + yy
            wait(chunks(far), wrecv.at[far])
            pass_mate(far)
            low, high = ((z + 6) % 8) * 8 + yy, ((z + 2) % 8) * 8 + yy
            wait(env.at[low], erecv.at[low])
            pass_env(low, ZUP, zup)
            wait(env.at[high], erecv.at[high])
            pass_env(high, ZDOWN, zdown)

        @pl.when(jnp.logical_and(i >= 3, i < 11))
        def _():
            yy = source(i - 3)
            even = yy % 2 == 0
            low, high = ((z + 5) % 8) * 8 + yy, ((z + 3) % 8) * 8 + yy
            wait(env.at[low], erecv.at[low])

            @pl.when(even)
            def _():
                pass_env(low, ZUP, zup)

            wait(env.at[high], erecv.at[high])

            @pl.when(jnp.logical_not(even))
            def _():
                pass_env(high, ZDOWN, zdown)

        @pl.when(i >= 4)
        def _():
            far = ((z + 4) % 8) * 8 + source(i - 4)
            wait(env.at[far], erecv.at[far])

        return carry

    lax.fori_loop(0, 12, turn, 0)

    wait(lists_vmem, lists_recv)
    load = pltpu.make_async_copy(lists_vmem, lists, lists_recv)
    load.start()
    wait(chunks(mine), wrecv.at[mine])
    wait(chunks(0, 32), mate_recv)
    load.wait()

    def left_pair(p, total):
        one, two = lists[0, 2 * p], lists[0, 2 * p + 1]
        lhs = jnp.concatenate([env[(one >> 8) & 63, 0], env[(two >> 8) & 63, 0]], axis=1)
        rhs = jnp.concatenate(
            [
                jnp.concatenate([wave[one & 255, 0], wave[one & 255, 1]], axis=1),
                jnp.concatenate([wave[two & 255, 0], wave[two & 255, 1]], axis=1),
            ],
            axis=0,
        )
        product = jnp.dot(lhs, rhs, preferred_element_type=jnp.float32)
        total = product + total * (one >> 16).astype(jnp.float32)
        inter[p, 0] = total[:, :128].astype(jnp.bfloat16)
        inter[p, 1] = total[:, 128:].astype(jnp.bfloat16)
        return total

    lax.fori_loop(0, LEFT_PAIRS, left_pair, jnp.zeros((128, 256), jnp.float32), unroll=8)

    def right_pair(p, total):
        row, column = 1 + p // 64, 2 * (p % 64)
        one, two = lists[row, column], lists[row, column + 1]
        lhs = jnp.concatenate(
            [
                inter[(one >> 8) & 127].reshape(256, 128),
                inter[(two >> 8) & 127].reshape(256, 128),
            ],
            axis=1,
        )
        rhs = jnp.concatenate([env[one & 63, 1], env[two & 63, 1]], axis=0)
        product = jnp.dot(lhs, rhs, preferred_element_type=jnp.float32)
        total = product + total * (one >> 16).astype(jnp.float32)
        cumulated[p] = total.astype(jnp.bfloat16)
        return total

    lax.fori_loop(0, RIGHT_PAIRS, right_pair, jnp.zeros((256, 128), jnp.float32), unroll=8)
    for k in range(TILES):
        tile = cumulated[lists[4, k]].reshape(2, 8, 16, 128)
        partial[:, k] = jnp.swapaxes(tile, 0, 1)

    copies = []
    for h in range(STEPS):
        some = pl.ds(TILES // STEPS * h, TILES // STEPS)
        for k in (4, 5, 3, 6, 2, 7, 1):
            copy = pltpu.make_async_remote_copy(
                src_ref=partial.at[(xc + k) % 8, some], dst_ref=parts.at[k, some],
                send_sem=part_send.at[8 * h + k], recv_sem=recv.at[8 * h + k],
                device_id=peers[k - 1], device_id_type=MESH,
            )
            copy.start()
            copies.append(copy)
    for h in range(STEPS):
        some = pl.ds(TILES // STEPS * h, TILES // STEPS)
        for copy in copies[7 * h : 7 * h + 7]:
            copy.wait_recv()
        total = partial[xc, some].astype(jnp.float32)
        for k in range(1, 8):
            total += parts[k, some].astype(jnp.float32)
        result[some] = total.astype(jnp.bfloat16)

        @pl.when(fixed)
        def _():
            pltpu.make_async_copy(result.at[some], out.at[some], last_recv.at[h]).start()

        @pl.when(jnp.logical_not(fixed))
        def _():
            pltpu.make_async_remote_copy(
                src_ref=result.at[some], dst_ref=out.at[some],
                send_sem=last_send.at[h], recv_sem=last_recv.at[h],
                device_id=partner, device_id_type=MESH,
            ).start()

    wait(chunks(0, 7), send.at[Y_SEND])
    wait(env.at[pl.ds(0, 7)], send.at[EY_SEND])
    wait(chunks(0, 32), send.at[MATE_SEND])
    wait(chunks(0, 12), send.at[XUP])
    wait(chunks(0, 12), send.at[XDOWN])
    wait(env.at[pl.ds(0, 28)], send.at[ZUP])
    wait(env.at[pl.ds(0, 28)], send.at[ZDOWN])
    for copy in copies:
        copy.wait_send()

    @pl.when(jnp.logical_not(fixed))
    def _():
        wait(env.at[0], send.at[E_SEND])
        wait(lists_vmem, send.at[LISTS_SEND])
        for h in range(STEPS):
            wait(result.at[pl.ds(0, TILES // STEPS)], last_send.at[h])

    for h in range(STEPS):
        wait(result.at[pl.ds(0, TILES // STEPS)], last_recv.at[h])


def main(*operands):
    return pl.pallas_call(
        main_kernel,
        out_shape=jax.ShapeDtypeStruct((TILES, 2, 16, 128), jnp.bfloat16),
        in_specs=[ANY, SMEM, ANY, ANY, VMEM, VMEM],
        out_specs=VMEM,
        scratch_shapes=[
            pltpu.VMEM((16, 2, 128, 128), jnp.bfloat16),
            pltpu.VMEM((16, 2, 128, 128), jnp.bfloat16),
            pltpu.VMEM((8, 128), jnp.int32),
            pltpu.VMEM((8, 128), jnp.int32),
            pltpu.SMEM((8, 128), jnp.int32),
            pltpu.VMEM((129, 2, 128, 128), jnp.bfloat16),
            pltpu.VMEM((64, 2, 128, 128), jnp.bfloat16),
            pltpu.VMEM((LEFT_PAIRS + 1, 2, 128, 128), jnp.bfloat16),
            pltpu.VMEM((RIGHT_PAIRS + 1, 256, 128), jnp.bfloat16),
            pltpu.VMEM((8, TILES, 2, 16, 128), jnp.bfloat16),
            pltpu.VMEM((8, TILES, 2, 16, 128), jnp.bfloat16),
            pltpu.VMEM((TILES, 2, 16, 128), jnp.bfloat16),
            pltpu.SemaphoreType.DMA((64,)),
            pltpu.SemaphoreType.DMA((64,)),
            pltpu.SemaphoreType.DMA,
            pltpu.SemaphoreType.DMA,
            pltpu.SemaphoreType.DMA((9,)),
            pltpu.SemaphoreType.DMA((8 * STEPS,)),
            pltpu.SemaphoreType.DMA((8 * STEPS,)),
            pltpu.SemaphoreType.DMA((STEPS,)),
            pltpu.SemaphoreType.DMA((STEPS,)),
            pltpu.SemaphoreType.DMA,
        ],
        compiler_params=pltpu.CompilerParams(
            collective_id=0, has_side_effects=True, vmem_limit_bytes=60 << 20
        ),
        name="main",
    )(*operands)


def shards(wave_tiles, left_env, right_env, send_list, left_tasks, right_tasks):
    rows = main(
        wave_tiles,
        send_list,
        left_env[0, 0],
        right_env[0, 0],
        jnp.transpose(left_tasks[0], (2, 0, 1)),
        jnp.transpose(right_tasks[0], (2, 0, 1)),
    )
    return rows.astype(jnp.float32)


def solution(mesh):
    fine = Mesh(mesh.devices.reshape(8, 4, 8, 2), AXES)
    sector = ("x", "y", "core")
    in_specs = (
        P(sector, None, None, None),
        P("z", sector, None, None),
        P("z", sector, None, None),
        P(sector, None),
        P("z", sector, None, None),
        P("z", sector, None, None),
    )
    out_specs = P(sector, None, "z", None)
    return jax.shard_map(shards, mesh=fine, in_specs=in_specs, out_specs=out_specs, check_vma=False)
```

```python
import jax
import jax.numpy as jnp
from jax import lax
from jax.experimental import pallas as pl
from jax.experimental.pallas import tpu as pltpu
from jax.sharding import Mesh
from jax.sharding import PartitionSpec as P

TILES = 16
LEFT_PAIRS = 64
RIGHT_PAIRS = 136
STEPS = 4
AXES = ("z", "x", "y", "core")
MESH = pl.DeviceIdType.MESH
ANY = pl.BlockSpec(memory_space=pl.ANY)
VMEM = pl.BlockSpec(memory_space=pltpu.VMEM)
SMEM = pl.BlockSpec(memory_space=pltpu.SMEM)


def place():
    return tuple(lax.axis_index(name) for name in AXES)


def swapped(z, x, y, c):
    return (2 * x + c, z // 2, y, z % 2)


def build_lists(left, right, lists):
    def iota(shape, axis):
        return lax.broadcasted_iota(jnp.int32, shape, axis)

    def total(mask, value, axis):
        return jnp.sum(jnp.where(mask, value, 0), axis=axis, keepdims=True)

    def column(row):
        n = row.shape[1]
        return total(iota((n, n), 0) == iota((n, n), 1), row, 1)

    def ordered(row):
        n = row.shape[1]
        down, across = iota((n, n), 0), iota((n, n), 1)
        key = column(row)
        same = key == row
        within = total(jnp.logical_and(same, across < down), 1, 1)
        later = total(jnp.logical_and(same, across > down), 1, 1)
        within_row = total(jnp.logical_and(same, down < across), 1, 0)
        start = total(row < key, 1 - (within_row & 1), 1)
        return key, within, 2 * start + within, later == 0

    def env_place(e):
        return ((e >> 4) << 4) | ((e & 1) << 3) | ((e >> 1) & 7)

    key, within, spot, last = ordered(left[2])
    slot = left[1]
    sender = slot >> 1
    source = ((((sender >> 4) << 1) | (sender & 1)) << 4) | (((sender >> 1) & 7) << 1) | (slot & 1)
    value = column(env_place(left[0]) * 256 + source) + jnp.where(within > 0, 65536, 0)
    n = left.shape[2]
    lists[0:1] = 128 + total(spot == iota((n, 128), 1), value - 128, 0)
    n_right = right.shape[2]
    hit = jnp.logical_and(key == right[0], last)
    made = LEFT_PAIRS + total(hit, (spot >> 1) - LEFT_PAIRS, 0)
    key, within, spot, last = ordered(right[2])
    value = column(made * 256 + env_place(right[1])) + jnp.where(within > 0, 65536, 0)
    empty = LEFT_PAIRS * 256
    for part in range(3):
        place = iota((n_right, 128), 1) + 128 * part
        lists[1 + part : 2 + part] = empty + total(spot == place, value - empty, 0)
    hit = jnp.logical_and(key == iota((n_right, 128), 1), last)
    lists[4:5] = RIGHT_PAIRS + total(hit, (spot >> 1) - RIGHT_PAIRS, 0)
    lists[5:8] = jnp.zeros((3, 128), jnp.int32)


def main_kernel(
    wave_in, picks, left_in, right_in, left_tasks, right_tasks, out,
    tiles, outgoing, lists_in, lists_vmem, lists, wave, env, inter,
    cumulated, partial, theirs, pair, parts, result,
    wrecv, erecv, mate_recv, lists_recv, send, theirs_recv, theirs_send,
    recv, part_send, last_recv, last_send, tiles_recv,
):
    z, x, y, c = place()
    xc = 2 * x + c
    fixed = z == xc
    partner = swapped(z, x, y, c)
    mate = (z, x, y, 1 - c)
    xup, xdown = (z, (x + 1) % 4, y, c), (z, (x + 3) % 4, y, c)
    zup, zdown = ((z + 1) % 8, x, y, c), ((z + 7) % 8, x, y, c)
    lane = [(z, (x + k) % 4, y, c) for k in range(1, 4)]

    fetch = pltpu.make_async_copy(wave_in, tiles, tiles_recv)
    fetch.start()
    barrier = pltpu.get_barrier_semaphore()
    for peer in lane + [mate, zup, zdown] + [(z, x, (y + d) % 8, c) for d in range(1, 8)]:
        pl.semaphore_signal(barrier, inc=1, device_id=peer, device_id_type=MESH)

    @pl.when(jnp.logical_not(fixed))
    def _():
        pl.semaphore_signal(barrier, inc=1, device_id=partner, device_id_type=MESH)

    wave[128] = jnp.zeros((2, 128, 128), jnp.bfloat16)
    inter[LEFT_PAIRS] = jnp.zeros((2, 128, 128), jnp.bfloat16)
    cumulated[RIGHT_PAIRS] = jnp.zeros((256, 128), jnp.float32)
    fetch.wait()
    for to in range(8):
        owner = (z // 2 * 8 + to) * 2 + z % 2
        for slot in range(2):
            index = picks[0, 2 * owner + slot]
            tile = tiles[jnp.maximum(index, 0)]
            outgoing[2 * to + slot] = jnp.where(index >= 0, tile, jnp.zeros_like(tile))

    pl.semaphore_wait(barrier, 13 + jnp.where(fixed, 0, 1))
    Y_SEND, EY_SEND, MATE_SEND, XUP, XDOWN, ZUP, ZDOWN, E_SEND, LISTS_SEND = range(9)

    def remote(source, target, sender, receiver, device):
        pltpu.make_async_remote_copy(
            src_ref=source, dst_ref=target, send_sem=send.at[sender], recv_sem=receiver,
            device_id=device, device_id_type=MESH,
        ).start()

    def wait(ref, sem):
        pltpu.make_async_copy(ref, ref, sem).wait()

    def chunks(slot, count=1):
        return wave.at[pl.ds(2 * slot, 2 * count)]

    def pass_wave(slot, sender, device):
        remote(chunks(slot), chunks(slot), sender, wrecv.at[slot], device)

    def pass_mate(slot):
        remote(chunks(slot), chunks(slot), MATE_SEND, mate_recv, mate)

    def pass_env(slot, sender, device):
        remote(env.at[slot], env.at[slot], sender, erecv.at[slot], device)

    mine = xc * 8 + y

    @pl.when(fixed)
    def _():
        pltpu.make_async_copy(left_in, env.at[mine, 0], erecv.at[mine]).start()
        pltpu.make_async_copy(right_in, env.at[mine, 1], erecv.at[mine]).start()

    @pl.when(jnp.logical_not(fixed))
    def _():
        remote(left_in, env.at[mine, 0], E_SEND, erecv.at[mine], partner)
        remote(right_in, env.at[mine, 1], E_SEND, erecv.at[mine], partner)

    own = z * 8 + y

    def shift(r):
        step = (r + 1) // 2
        return jnp.where(r % 2 == 1, step, 8 - step)

    def send_wave(r):
        to = (y + 8 - shift(r)) % 8
        remote(outgoing.at[pl.ds(2 * to, 2)], chunks(mine), Y_SEND, wrecv.at[mine], (z, x, to, c))

    def send_env(r):
        to = (y + 8 - shift(r)) % 8
        remote(env.at[own], env.at[own], EY_SEND, erecv.at[own], (z, x, to, c))

    here = outgoing.at[pl.ds(2 * y, 2)]
    pltpu.make_async_copy(here, chunks(mine), wrecv.at[mine]).start()
    for r in range(1, 5):
        send_wave(r)
    remote(here, chunks(mine), XUP, wrecv.at[mine], xup)
    remote(here, chunks(mine), XDOWN, wrecv.at[mine], xdown)
    remote(here, chunks(mine), MATE_SEND, mate_recv, mate)
    build_lists(left_tasks, right_tasks, lists_in)

    @pl.when(fixed)
    def _():
        pltpu.make_async_copy(lists_in, lists_vmem, lists_recv).start()

    @pl.when(jnp.logical_not(fixed))
    def _():
        remote(lists_in, lists_vmem, LISTS_SEND, lists_recv, partner)

    wait(env.at[own], erecv.at[own])
    for r in range(1, 5):
        send_env(r)

    def source(r):
        return (y + shift(r)) % 8

    def turn(i, carry):
        @pl.when(i < 3)
        def _():
            send_env(i + 5)
            send_wave(i + 5)

        @pl.when(i < 8)
        def _():
            yy = source(i)
            slot = xc * 8 + yy

            @pl.when(i > 0)
            def _():
                wait(chunks(slot), wrecv.at[slot])
                pass_wave(slot, XUP, xup)
                pass_wave(slot, XDOWN, xdown)
                pass_mate(slot)

            slot = z * 8 + yy

            @pl.when(i > 0)
            def _():
                wait(env.at[slot], erecv.at[slot])

            pass_env(slot, ZUP, zup)
            pass_env(slot, ZDOWN, zdown)

        @pl.when(jnp.logical_and(i >= 1, i < 9))
        def _():
            yy = source(i - 1)
            even = yy % 2 == 0
            low = (2 * ((x + 3) % 4) + c) * 8 + yy
            wait(chunks(low), wrecv.at[low])

            @pl.when(even)
            def _():
                pass_wave(low, XUP, xup)

            pass_mate(low)
            high = (2 * ((x + 1) % 4) + c) * 8 + yy
            wait(chunks(high), wrecv.at[high])

            @pl.when(jnp.logical_not(even))
            def _():
                pass_wave(high, XDOWN, xdown)

            pass_mate(high)
            low, high = ((z + 7) % 8) * 8 + yy, ((z + 1) % 8) * 8 + yy
            wait(env.at[low], erecv.at[low])
            pass_env(low, ZUP, zup)
            wait(env.at[high], erecv.at[high])
            pass_env(high, ZDOWN, zdown)

        @pl.when(jnp.logical_and(i >= 2, i < 10))
        def _():
            yy = source(i - 2)
            far = (2 * ((x + 2) % 4) + c) * 8 + yy
            wait(chunks(far), wrecv.at[far])
            pass_mate(far)
            low, high = ((z + 6) % 8) * 8 + yy, ((z + 2) % 8) * 8 + yy
            wait(env.at[low], erecv.at[low])
            pass_env(low, ZUP, zup)
            wait(env.at[high], erecv.at[high])
            pass_env(high, ZDOWN, zdown)

        @pl.when(jnp.logical_and(i >= 3, i < 11))
        def _():
            yy = source(i - 3)
            even = yy % 2 == 0
            low, high = ((z + 5) % 8) * 8 + yy, ((z + 3) % 8) * 8 + yy
            wait(env.at[low], erecv.at[low])

            @pl.when(even)
            def _():
                pass_env(low, ZUP, zup)

            wait(env.at[high], erecv.at[high])

            @pl.when(jnp.logical_not(even))
            def _():
                pass_env(high, ZDOWN, zdown)

        @pl.when(i >= 4)
        def _():
            far = ((z + 4) % 8) * 8 + source(i - 4)
            wait(env.at[far], erecv.at[far])

        return carry

    lax.fori_loop(0, 12, turn, 0)

    wait(lists_vmem, lists_recv)
    load = pltpu.make_async_copy(lists_vmem, lists, lists_recv)
    load.start()
    wait(chunks(mine), wrecv.at[mine])
    wait(chunks(0, 32), mate_recv)
    load.wait()

    def left_pair(p, total):
        one, two = lists[0, 2 * p], lists[0, 2 * p + 1]
        lhs = jnp.concatenate([env[(one >> 8) & 63, 0], env[(two >> 8) & 63, 0]], axis=1)
        rhs = jnp.concatenate(
            [
                jnp.concatenate([wave[one & 255, 0], wave[one & 255, 1]], axis=1),
                jnp.concatenate([wave[two & 255, 0], wave[two & 255, 1]], axis=1),
            ],
            axis=0,
        )
        product = jnp.dot(lhs, rhs, preferred_element_type=jnp.float32)
        total = product + total * (one >> 16).astype(jnp.float32)
        inter[p, 0] = total[:, :128].astype(jnp.bfloat16)
        inter[p, 1] = total[:, 128:].astype(jnp.bfloat16)
        return total

    lax.fori_loop(0, LEFT_PAIRS, left_pair, jnp.zeros((128, 256), jnp.float32), unroll=16)

    def right_pair(p, total):
        row, column = 1 + p // 64, 2 * (p % 64)
        one, two = lists[row, column], lists[row, column + 1]
        lhs = jnp.concatenate(
            [
                inter[(one >> 8) & 127].reshape(256, 128),
                inter[(two >> 8) & 127].reshape(256, 128),
            ],
            axis=1,
        )
        rhs = jnp.concatenate([env[one & 63, 1], env[two & 63, 1]], axis=0)
        product = jnp.dot(lhs, rhs, preferred_element_type=jnp.float32)
        total = product + total * (one >> 16).astype(jnp.float32)
        cumulated[p] = total
        return total

    lax.fori_loop(0, RIGHT_PAIRS, right_pair, jnp.zeros((256, 128), jnp.float32), unroll=17)

    def block(h):
        return pl.ds(TILES // STEPS * h, TILES // STEPS)

    def to_mate(h):
        return pltpu.make_async_remote_copy(
            src_ref=partial.at[1 - c, :, block(h)], dst_ref=theirs.at[:, block(h)],
            send_sem=theirs_send.at[h], recv_sem=theirs_recv.at[h],
            device_id=mate, device_id_type=MESH,
        )

    def to_chip(h, k):
        return pltpu.make_async_remote_copy(
            src_ref=pair.at[(x + k) % 4, block(h)], dst_ref=parts.at[k - 1, block(h)],
            send_sem=part_send.at[4 * h + k], recv_sem=recv.at[4 * h + k],
            device_id=lane[k - 1], device_id_type=MESH,
        )

    for h in range(STEPS):
        for k in range(TILES // STEPS * h, TILES // STEPS * (h + 1)):
            tile = cumulated[lists[4, k]].reshape(2, 8, 16, 128)
            for t in range(8):
                partial[t % 2, t // 2, k] = tile[:, t]
        to_mate(h).start()
    for h in range(STEPS):
        to_mate(h).wait_recv()
        pair[:, block(h)] = (partial[c, :, block(h)] + theirs[:, block(h)]).astype(jnp.bfloat16)
        for k in (2, 1, 3):
            to_chip(h, k).start()
    for h in range(STEPS):
        total = partial[c, x, block(h)] + theirs[x, block(h)]
        for k in (1, 2, 3):
            to_chip(h, k).wait_recv()
            total += parts[k - 1, block(h)].astype(jnp.float32)
        result[block(h)] = total.astype(jnp.bfloat16)

        @pl.when(fixed)
        def _():
            pltpu.make_async_copy(result.at[block(h)], out.at[block(h)], last_recv.at[h]).start()

        @pl.when(jnp.logical_not(fixed))
        def _():
            pltpu.make_async_remote_copy(
                src_ref=result.at[block(h)], dst_ref=out.at[block(h)],
                send_sem=last_send.at[h], recv_sem=last_recv.at[h],
                device_id=partner, device_id_type=MESH,
            ).start()

    wait(chunks(0, 7), send.at[Y_SEND])
    wait(env.at[pl.ds(0, 7)], send.at[EY_SEND])
    wait(chunks(0, 32), send.at[MATE_SEND])
    wait(chunks(0, 12), send.at[XUP])
    wait(chunks(0, 12), send.at[XDOWN])
    wait(env.at[pl.ds(0, 28)], send.at[ZUP])
    wait(env.at[pl.ds(0, 28)], send.at[ZDOWN])
    for h in range(STEPS):
        to_mate(h).wait_send()
        for k in (1, 2, 3):
            to_chip(h, k).wait_send()

    @pl.when(jnp.logical_not(fixed))
    def _():
        wait(env.at[0], send.at[E_SEND])
        wait(lists_vmem, send.at[LISTS_SEND])
        for h in range(STEPS):
            wait(result.at[pl.ds(0, TILES // STEPS)], last_send.at[h])

    for h in range(STEPS):
        wait(result.at[pl.ds(0, TILES // STEPS)], last_recv.at[h])


def main(*operands):
    return pl.pallas_call(
        main_kernel,
        out_shape=jax.ShapeDtypeStruct((TILES, 2, 16, 128), jnp.bfloat16),
        in_specs=[ANY, SMEM, ANY, ANY, VMEM, VMEM],
        out_specs=VMEM,
        scratch_shapes=[
            pltpu.VMEM((16, 2, 128, 128), jnp.bfloat16),
            pltpu.VMEM((16, 2, 128, 128), jnp.bfloat16),
            pltpu.VMEM((8, 128), jnp.int32),
            pltpu.VMEM((8, 128), jnp.int32),
            pltpu.SMEM((8, 128), jnp.int32),
            pltpu.VMEM((129, 2, 128, 128), jnp.bfloat16),
            pltpu.VMEM((64, 2, 128, 128), jnp.bfloat16),
            pltpu.VMEM((LEFT_PAIRS + 1, 2, 128, 128), jnp.bfloat16),
            pltpu.VMEM((RIGHT_PAIRS + 1, 256, 128), jnp.float32),
            pltpu.VMEM((2, 4, TILES, 2, 16, 128), jnp.float32),
            pltpu.VMEM((4, TILES, 2, 16, 128), jnp.float32),
            pltpu.VMEM((4, TILES, 2, 16, 128), jnp.bfloat16),
            pltpu.VMEM((3, TILES, 2, 16, 128), jnp.bfloat16),
            pltpu.VMEM((TILES, 2, 16, 128), jnp.bfloat16),
            pltpu.SemaphoreType.DMA((64,)),
            pltpu.SemaphoreType.DMA((64,)),
            pltpu.SemaphoreType.DMA,
            pltpu.SemaphoreType.DMA,
            pltpu.SemaphoreType.DMA((9,)),
            pltpu.SemaphoreType.DMA((STEPS,)),
            pltpu.SemaphoreType.DMA((STEPS,)),
            pltpu.SemaphoreType.DMA((4 * STEPS,)),
            pltpu.SemaphoreType.DMA((4 * STEPS,)),
            pltpu.SemaphoreType.DMA((STEPS,)),
            pltpu.SemaphoreType.DMA((STEPS,)),
            pltpu.SemaphoreType.DMA,
        ],
        compiler_params=pltpu.CompilerParams(
            collective_id=0, has_side_effects=True, vmem_limit_bytes=60 << 20
        ),
        name="main",
    )(*operands)


def shards(wave_tiles, left_env, right_env, send_list, left_tasks, right_tasks):
    rows = main(
        wave_tiles,
        send_list,
        left_env[0, 0],
        right_env[0, 0],
        jnp.transpose(left_tasks[0], (2, 0, 1)),
        jnp.transpose(right_tasks[0], (2, 0, 1)),
    )
    return rows.astype(jnp.float32)


def solution(mesh):
    fine = Mesh(mesh.devices.reshape(8, 4, 8, 2), AXES)
    sector = ("x", "y", "core")
    in_specs = (
        P(sector, None, None, None),
        P("z", sector, None, None),
        P("z", sector, None, None),
        P(sector, None),
        P("z", sector, None, None),
        P("z", sector, None, None),
    )
    out_specs = P(sector, None, "z", None)
    return jax.shard_map(shards, mesh=fine, in_specs=in_specs, out_specs=out_specs, check_vma=False)
```

```python
import jax
import jax.numpy as jnp
from jax import lax
from jax.experimental import pallas as pl
from jax.experimental.pallas import tpu as pltpu
from jax.sharding import Mesh
from jax.sharding import PartitionSpec as P

TILES = 16
LEFT_PAIRS = 64
RIGHT_PAIRS = 136
STEPS = 4
AXES = ("z", "x", "y", "core")
MESH = pl.DeviceIdType.MESH
ANY = pl.BlockSpec(memory_space=pl.ANY)
VMEM = pl.BlockSpec(memory_space=pltpu.VMEM)
SMEM = pl.BlockSpec(memory_space=pltpu.SMEM)


def place():
    return tuple(lax.axis_index(name) for name in AXES)


def swapped(z, x, y, c):
    return (2 * x + c, z // 2, y, z % 2)


def build_lists(left, right, lists):
    def iota(shape, axis):
        return lax.broadcasted_iota(jnp.int32, shape, axis)

    def total(mask, value, axis):
        return jnp.sum(jnp.where(mask, value, 0), axis=axis, keepdims=True)

    def column(row):
        n = row.shape[1]
        return total(iota((n, n), 0) == iota((n, n), 1), row, 1)

    def ordered(row):
        n = row.shape[1]
        down, across = iota((n, n), 0), iota((n, n), 1)
        key = column(row)
        same = key == row
        within = total(jnp.logical_and(same, across < down), 1, 1)
        later = total(jnp.logical_and(same, across > down), 1, 1)
        within_row = total(jnp.logical_and(same, down < across), 1, 0)
        start = total(row < key, 1 - (within_row & 1), 1)
        return key, within, 2 * start + within, later == 0

    def env_place(e):
        return ((e >> 4) << 4) | ((e & 1) << 3) | ((e >> 1) & 7)

    key, within, spot, last = ordered(left[2])
    slot = left[1]
    sender = slot >> 1
    source = ((((sender >> 4) << 1) | (sender & 1)) << 4) | (((sender >> 1) & 7) << 1) | (slot & 1)
    value = column(env_place(left[0]) * 256 + source) + jnp.where(within > 0, 65536, 0)
    n = left.shape[2]
    lists[0:1] = 128 + total(spot == iota((n, 128), 1), value - 128, 0)
    n_right = right.shape[2]
    hit = jnp.logical_and(key == right[0], last)
    made = LEFT_PAIRS + total(hit, (spot >> 1) - LEFT_PAIRS, 0)
    key, within, spot, last = ordered(right[2])
    value = column(made * 256 + env_place(right[1])) + jnp.where(within > 0, 65536, 0)
    empty = LEFT_PAIRS * 256
    for part in range(3):
        place = iota((n_right, 128), 1) + 128 * part
        lists[1 + part : 2 + part] = empty + total(spot == place, value - empty, 0)
    hit = jnp.logical_and(key == iota((n_right, 128), 1), last)
    lists[4:5] = RIGHT_PAIRS + total(hit, (spot >> 1) - RIGHT_PAIRS, 0)
    lists[5:8] = jnp.zeros((3, 128), jnp.int32)


def main_kernel(
    wave_in, picks, left_in, right_in, left_tasks, right_tasks, out,
    tiles, outgoing, lists_in, lists_vmem, lists, wave, env, inter,
    cumulated, partial, theirs, pair, parts, result,
    wrecv, erecv, mate_recv, lists_recv, send, theirs_recv, theirs_send,
    recv, part_send, last_recv, last_send, tiles_recv,
):
    z, x, y, c = place()
    xc = 2 * x + c
    fixed = z == xc
    partner = swapped(z, x, y, c)
    mate = (z, x, y, 1 - c)
    xup, xdown = (z, (x + 1) % 4, y, c), (z, (x + 3) % 4, y, c)
    zup, zdown = ((z + 1) % 8, x, y, c), ((z + 7) % 8, x, y, c)
    lane = [(z, (x + k) % 4, y, c) for k in range(1, 4)]

    fetch = pltpu.make_async_copy(wave_in, tiles, tiles_recv)
    fetch.start()
    barrier = pltpu.get_barrier_semaphore()
    for peer in lane + [mate, zup, zdown] + [(z, x, (y + d) % 8, c) for d in range(1, 8)]:
        pl.semaphore_signal(barrier, inc=1, device_id=peer, device_id_type=MESH)

    @pl.when(jnp.logical_not(fixed))
    def _():
        pl.semaphore_signal(barrier, inc=1, device_id=partner, device_id_type=MESH)

    wave[128] = jnp.zeros((2, 128, 128), jnp.bfloat16)
    inter[LEFT_PAIRS] = jnp.zeros((2, 128, 128), jnp.bfloat16)
    cumulated[RIGHT_PAIRS] = jnp.zeros((256, 128), jnp.float32)
    fetch.wait()
    for to in range(8):
        owner = (z // 2 * 8 + to) * 2 + z % 2
        for slot in range(2):
            index = picks[0, 2 * owner + slot]
            tile = tiles[jnp.maximum(index, 0)]
            outgoing[2 * to + slot] = jnp.where(index >= 0, tile, jnp.zeros_like(tile))

    pl.semaphore_wait(barrier, 13 + jnp.where(fixed, 0, 1))
    Y_SEND, EY_SEND, MATE_SEND, XUP, XDOWN, ZUP, ZDOWN, E_SEND, LISTS_SEND = range(9)

    def remote(source, target, sender, receiver, device):
        pltpu.make_async_remote_copy(
            src_ref=source, dst_ref=target, send_sem=send.at[sender], recv_sem=receiver,
            device_id=device, device_id_type=MESH,
        ).start()

    def wait(ref, sem):
        pltpu.make_async_copy(ref, ref, sem).wait()

    def chunks(slot, count=1):
        return wave.at[pl.ds(2 * slot, 2 * count)]

    def pass_wave(slot, sender, device):
        remote(chunks(slot), chunks(slot), sender, wrecv.at[slot], device)

    def pass_mate(slot):
        remote(chunks(slot), chunks(slot), MATE_SEND, mate_recv, mate)

    def pass_env(slot, sender, device):
        remote(env.at[slot], env.at[slot], sender, erecv.at[slot], device)

    mine = xc * 8 + y

    @pl.when(fixed)
    def _():
        pltpu.make_async_copy(left_in, env.at[mine, 0], erecv.at[mine]).start()
        pltpu.make_async_copy(right_in, env.at[mine, 1], erecv.at[mine]).start()

    @pl.when(jnp.logical_not(fixed))
    def _():
        remote(left_in, env.at[mine, 0], E_SEND, erecv.at[mine], partner)
        remote(right_in, env.at[mine, 1], E_SEND, erecv.at[mine], partner)

    own = z * 8 + y

    def shift(r):
        step = (r + 1) // 2
        return jnp.where(r % 2 == 1, step, 8 - step)

    def send_wave(r):
        to = (y + 8 - shift(r)) % 8
        remote(outgoing.at[pl.ds(2 * to, 2)], chunks(mine), Y_SEND, wrecv.at[mine], (z, x, to, c))

    def send_env(r):
        to = (y + 8 - shift(r)) % 8
        remote(env.at[own], env.at[own], EY_SEND, erecv.at[own], (z, x, to, c))

    here = outgoing.at[pl.ds(2 * y, 2)]
    pltpu.make_async_copy(here, chunks(mine), wrecv.at[mine]).start()
    for r in range(1, 5):
        send_wave(r)
    remote(here, chunks(mine), XUP, wrecv.at[mine], xup)
    remote(here, chunks(mine), XDOWN, wrecv.at[mine], xdown)
    remote(here, chunks(mine), MATE_SEND, mate_recv, mate)
    build_lists(left_tasks, right_tasks, lists_in)

    @pl.when(fixed)
    def _():
        pltpu.make_async_copy(lists_in, lists_vmem, lists_recv).start()

    @pl.when(jnp.logical_not(fixed))
    def _():
        remote(lists_in, lists_vmem, LISTS_SEND, lists_recv, partner)

    wait(env.at[own], erecv.at[own])
    for r in range(1, 5):
        send_env(r)

    def source(r):
        return (y + shift(r)) % 8

    def turn(i, carry):
        @pl.when(i < 3)
        def _():
            send_wave(i + 5)
            send_env(i + 5)

        @pl.when(i < 8)
        def _():
            yy = source(i)
            slot = xc * 8 + yy

            @pl.when(i > 0)
            def _():
                wait(chunks(slot), wrecv.at[slot])
                pass_wave(slot, XUP, xup)
                pass_wave(slot, XDOWN, xdown)
                pass_mate(slot)

            slot = z * 8 + yy

            @pl.when(i > 0)
            def _():
                wait(env.at[slot], erecv.at[slot])

            pass_env(slot, ZUP, zup)
            pass_env(slot, ZDOWN, zdown)

        @pl.when(jnp.logical_and(i >= 1, i < 9))
        def _():
            yy = source(i - 1)
            even = yy % 2 == 0
            low = (2 * ((x + 3) % 4) + c) * 8 + yy
            wait(chunks(low), wrecv.at[low])

            @pl.when(even)
            def _():
                pass_wave(low, XUP, xup)

            pass_mate(low)
            high = (2 * ((x + 1) % 4) + c) * 8 + yy
            wait(chunks(high), wrecv.at[high])

            @pl.when(jnp.logical_not(even))
            def _():
                pass_wave(high, XDOWN, xdown)

            pass_mate(high)
            low, high = ((z + 7) % 8) * 8 + yy, ((z + 1) % 8) * 8 + yy
            wait(env.at[low], erecv.at[low])
            pass_env(low, ZUP, zup)
            wait(env.at[high], erecv.at[high])
            pass_env(high, ZDOWN, zdown)

        @pl.when(jnp.logical_and(i >= 2, i < 10))
        def _():
            yy = source(i - 2)
            far = (2 * ((x + 2) % 4) + c) * 8 + yy
            wait(chunks(far), wrecv.at[far])
            pass_mate(far)
            low, high = ((z + 6) % 8) * 8 + yy, ((z + 2) % 8) * 8 + yy
            wait(env.at[low], erecv.at[low])
            pass_env(low, ZUP, zup)
            wait(env.at[high], erecv.at[high])
            pass_env(high, ZDOWN, zdown)

        @pl.when(jnp.logical_and(i >= 3, i < 11))
        def _():
            yy = source(i - 3)
            even = yy % 2 == 0
            low, high = ((z + 5) % 8) * 8 + yy, ((z + 3) % 8) * 8 + yy
            wait(env.at[low], erecv.at[low])

            @pl.when(even)
            def _():
                pass_env(low, ZUP, zup)

            wait(env.at[high], erecv.at[high])

            @pl.when(jnp.logical_not(even))
            def _():
                pass_env(high, ZDOWN, zdown)

        @pl.when(i >= 4)
        def _():
            far = ((z + 4) % 8) * 8 + source(i - 4)
            wait(env.at[far], erecv.at[far])

        return carry

    lax.fori_loop(0, 12, turn, 0)

    wait(lists_vmem, lists_recv)
    load = pltpu.make_async_copy(lists_vmem, lists, lists_recv)
    load.start()
    wait(chunks(mine), wrecv.at[mine])
    wait(chunks(0, 32), mate_recv)
    load.wait()

    def left_pair(p, total):
        one, two = lists[0, 2 * p], lists[0, 2 * p + 1]
        lhs = jnp.concatenate([env[(one >> 8) & 63, 0], env[(two >> 8) & 63, 0]], axis=1)
        rhs = jnp.concatenate(
            [
                jnp.concatenate([wave[one & 255, 0], wave[one & 255, 1]], axis=1),
                jnp.concatenate([wave[two & 255, 0], wave[two & 255, 1]], axis=1),
            ],
            axis=0,
        )
        product = jnp.dot(lhs, rhs, preferred_element_type=jnp.float32)
        total = product + total * (one >> 16).astype(jnp.float32)
        inter[p, 0] = total[:, :128].astype(jnp.bfloat16)
        inter[p, 1] = total[:, 128:].astype(jnp.bfloat16)
        return total

    lax.fori_loop(0, LEFT_PAIRS, left_pair, jnp.zeros((128, 256), jnp.float32), unroll=32)

    def right_pair(p, total):
        row, column = 1 + p // 64, 2 * (p % 64)
        one, two = lists[row, column], lists[row, column + 1]
        lhs = jnp.concatenate(
            [
                inter[(one >> 8) & 127].reshape(256, 128),
                inter[(two >> 8) & 127].reshape(256, 128),
            ],
            axis=1,
        )
        rhs = jnp.concatenate([env[one & 63, 1], env[two & 63, 1]], axis=0)
        product = jnp.dot(lhs, rhs, preferred_element_type=jnp.float32)
        total = product + total * (one >> 16).astype(jnp.float32)
        cumulated[p] = total
        return total

    lax.fori_loop(0, RIGHT_PAIRS, right_pair, jnp.zeros((256, 128), jnp.float32), unroll=34)

    def block(h):
        return pl.ds(TILES // STEPS * h, TILES // STEPS)

    def to_mate(h):
        return pltpu.make_async_remote_copy(
            src_ref=partial.at[1 - c, :, block(h)], dst_ref=theirs.at[:, block(h)],
            send_sem=theirs_send.at[h], recv_sem=theirs_recv.at[h],
            device_id=mate, device_id_type=MESH,
        )

    def to_chip(h, k):
        return pltpu.make_async_remote_copy(
            src_ref=pair.at[(x + k) % 4, block(h)], dst_ref=parts.at[k - 1, block(h)],
            send_sem=part_send.at[4 * h + k], recv_sem=recv.at[4 * h + k],
            device_id=lane[k - 1], device_id_type=MESH,
        )

    for h in range(STEPS):
        for k in range(TILES // STEPS * h, TILES // STEPS * (h + 1)):
            tile = cumulated[lists[4, k]].reshape(2, 8, 16, 128)
            for t in range(8):
                partial[t % 2, t // 2, k] = tile[:, t]
        to_mate(h).start()
    for h in range(STEPS):
        to_mate(h).wait_recv()
        pair[:, block(h)] = (partial[c, :, block(h)] + theirs[:, block(h)]).astype(jnp.bfloat16)
        for k in (2, 1, 3):
            to_chip(h, k).start()
    for h in range(STEPS):
        total = partial[c, x, block(h)] + theirs[x, block(h)]
        for k in (1, 2, 3):
            to_chip(h, k).wait_recv()
            total += parts[k - 1, block(h)].astype(jnp.float32)
        result[block(h)] = total.astype(jnp.bfloat16)

        @pl.when(fixed)
        def _():
            pltpu.make_async_copy(result.at[block(h)], out.at[block(h)], last_recv.at[h]).start()

        @pl.when(jnp.logical_not(fixed))
        def _():
            pltpu.make_async_remote_copy(
                src_ref=result.at[block(h)], dst_ref=out.at[block(h)],
                send_sem=last_send.at[h], recv_sem=last_recv.at[h],
                device_id=partner, device_id_type=MESH,
            ).start()

    wait(chunks(0, 7), send.at[Y_SEND])
    wait(env.at[pl.ds(0, 7)], send.at[EY_SEND])
    wait(chunks(0, 32), send.at[MATE_SEND])
    wait(chunks(0, 12), send.at[XUP])
    wait(chunks(0, 12), send.at[XDOWN])
    wait(env.at[pl.ds(0, 28)], send.at[ZUP])
    wait(env.at[pl.ds(0, 28)], send.at[ZDOWN])
    for h in range(STEPS):
        to_mate(h).wait_send()
        for k in (1, 2, 3):
            to_chip(h, k).wait_send()

    @pl.when(jnp.logical_not(fixed))
    def _():
        wait(env.at[0], send.at[E_SEND])
        wait(lists_vmem, send.at[LISTS_SEND])
        for h in range(STEPS):
            wait(result.at[pl.ds(0, TILES // STEPS)], last_send.at[h])

    for h in range(STEPS):
        wait(result.at[pl.ds(0, TILES // STEPS)], last_recv.at[h])


def main(*operands):
    return pl.pallas_call(
        main_kernel,
        out_shape=jax.ShapeDtypeStruct((TILES, 2, 16, 128), jnp.bfloat16),
        in_specs=[ANY, SMEM, ANY, ANY, VMEM, VMEM],
        out_specs=VMEM,
        scratch_shapes=[
            pltpu.VMEM((16, 2, 128, 128), jnp.bfloat16),
            pltpu.VMEM((16, 2, 128, 128), jnp.bfloat16),
            pltpu.VMEM((8, 128), jnp.int32),
            pltpu.VMEM((8, 128), jnp.int32),
            pltpu.SMEM((8, 128), jnp.int32),
            pltpu.VMEM((129, 2, 128, 128), jnp.bfloat16),
            pltpu.VMEM((64, 2, 128, 128), jnp.bfloat16),
            pltpu.VMEM((LEFT_PAIRS + 1, 2, 128, 128), jnp.bfloat16),
            pltpu.VMEM((RIGHT_PAIRS + 1, 256, 128), jnp.float32),
            pltpu.VMEM((2, 4, TILES, 2, 16, 128), jnp.float32),
            pltpu.VMEM((4, TILES, 2, 16, 128), jnp.float32),
            pltpu.VMEM((4, TILES, 2, 16, 128), jnp.bfloat16),
            pltpu.VMEM((3, TILES, 2, 16, 128), jnp.bfloat16),
            pltpu.VMEM((TILES, 2, 16, 128), jnp.bfloat16),
            pltpu.SemaphoreType.DMA((64,)),
            pltpu.SemaphoreType.DMA((64,)),
            pltpu.SemaphoreType.DMA,
            pltpu.SemaphoreType.DMA,
            pltpu.SemaphoreType.DMA((9,)),
            pltpu.SemaphoreType.DMA((STEPS,)),
            pltpu.SemaphoreType.DMA((STEPS,)),
            pltpu.SemaphoreType.DMA((4 * STEPS,)),
            pltpu.SemaphoreType.DMA((4 * STEPS,)),
            pltpu.SemaphoreType.DMA((STEPS,)),
            pltpu.SemaphoreType.DMA((STEPS,)),
            pltpu.SemaphoreType.DMA,
        ],
        compiler_params=pltpu.CompilerParams(
            collective_id=0, has_side_effects=True, vmem_limit_bytes=60 << 20
        ),
        name="main",
    )(*operands)


def shards(wave_tiles, left_env, right_env, send_list, left_tasks, right_tasks):
    rows = main(
        wave_tiles,
        send_list,
        left_env[0, 0],
        right_env[0, 0],
        jnp.transpose(left_tasks[0], (2, 0, 1)),
        jnp.transpose(right_tasks[0], (2, 0, 1)),
    )
    return rows.astype(jnp.float32)


def solution(mesh):
    fine = Mesh(mesh.devices.reshape(8, 4, 8, 2), AXES)
    sector = ("x", "y", "core")
    in_specs = (
        P(sector, None, None, None),
        P("z", sector, None, None),
        P("z", sector, None, None),
        P(sector, None),
        P("z", sector, None, None),
        P("z", sector, None, None),
    )
    out_specs = P(sector, None, "z", None)
    return jax.shard_map(shards, mesh=fine, in_specs=in_specs, out_specs=out_specs, check_vma=False)
```

```python
import jax
import jax.numpy as jnp
from jax import lax
from jax.experimental import pallas as pl
from jax.experimental.pallas import tpu as pltpu
from jax.sharding import Mesh
from jax.sharding import PartitionSpec as P

TILES = 16
LEFT_PAIRS = 64
RIGHT_PAIRS = 136
STEPS = 4
AXES = ("z", "x", "y", "core")
MESH = pl.DeviceIdType.MESH
ANY = pl.BlockSpec(memory_space=pl.ANY)
VMEM = pl.BlockSpec(memory_space=pltpu.VMEM)
SMEM = pl.BlockSpec(memory_space=pltpu.SMEM)


def place():
    return tuple(lax.axis_index(name) for name in AXES)


def swapped(z, x, y, c):
    return (2 * x + c, z // 2, y, z % 2)


def build_lists(left, right, lists):
    def iota(shape, axis):
        return lax.broadcasted_iota(jnp.int32, shape, axis)

    def total(mask, value, axis):
        return jnp.sum(jnp.where(mask, value, 0), axis=axis, keepdims=True)

    def column(row):
        n = row.shape[1]
        return total(iota((n, n), 0) == iota((n, n), 1), row, 1)

    def ordered(row):
        n = row.shape[1]
        down, across = iota((n, n), 0), iota((n, n), 1)
        key = column(row)
        same = key == row
        within = total(jnp.logical_and(same, across < down), 1, 1)
        later = total(jnp.logical_and(same, across > down), 1, 1)
        within_row = total(jnp.logical_and(same, down < across), 1, 0)
        start = total(row < key, 1 - (within_row & 1), 1)
        return key, within, 2 * start + within, later == 0

    def env_place(e):
        return ((e >> 4) << 4) | ((e & 1) << 3) | ((e >> 1) & 7)

    key, within, spot, last = ordered(left[2])
    slot = left[1]
    sender = slot >> 1
    source = ((((sender >> 4) << 1) | (sender & 1)) << 4) | (((sender >> 1) & 7) << 1) | (slot & 1)
    value = column(env_place(left[0]) * 256 + source) + jnp.where(within > 0, 65536, 0)
    n = left.shape[2]
    lists[0:1] = 128 + total(spot == iota((n, 128), 1), value - 128, 0)
    n_right = right.shape[2]
    hit = jnp.logical_and(key == right[0], last)
    made = LEFT_PAIRS + total(hit, (spot >> 1) - LEFT_PAIRS, 0)
    key, within, spot, last = ordered(right[2])
    value = column(made * 256 + env_place(right[1])) + jnp.where(within > 0, 65536, 0)
    empty = LEFT_PAIRS * 256
    for part in range(3):
        place = iota((n_right, 128), 1) + 128 * part
        lists[1 + part : 2 + part] = empty + total(spot == place, value - empty, 0)
    hit = jnp.logical_and(key == iota((n_right, 128), 1), last)
    lists[4:5] = RIGHT_PAIRS + total(hit, (spot >> 1) - RIGHT_PAIRS, 0)
    lists[5:8] = jnp.zeros((3, 128), jnp.int32)


def main_kernel(
    wave_in, picks, left_in, right_in, left_tasks, right_tasks, out,
    tiles, outgoing, lists_in, lists_vmem, lists, wave, env, inter,
    cumulated, partial, theirs, pair, parts, result,
    wrecv, erecv, mate_recv, lists_recv, send, theirs_recv, theirs_send,
    recv, part_send, last_recv, last_send, tiles_recv,
):
    z, x, y, c = place()
    xc = 2 * x + c
    fixed = z == xc
    partner = swapped(z, x, y, c)
    mate = (z, x, y, 1 - c)
    xup, xdown = (z, (x + 1) % 4, y, c), (z, (x + 3) % 4, y, c)
    zup, zdown = ((z + 1) % 8, x, y, c), ((z + 7) % 8, x, y, c)
    lane = [(z, (x + k) % 4, y, c) for k in range(1, 4)]

    fetch = pltpu.make_async_copy(wave_in, tiles, tiles_recv)
    fetch.start()
    barrier = pltpu.get_barrier_semaphore()
    for peer in lane + [mate, zup, zdown] + [(z, x, (y + d) % 8, c) for d in range(1, 8)]:
        pl.semaphore_signal(barrier, inc=1, device_id=peer, device_id_type=MESH)

    @pl.when(jnp.logical_not(fixed))
    def _():
        pl.semaphore_signal(barrier, inc=1, device_id=partner, device_id_type=MESH)

    wave[128] = jnp.zeros((2, 128, 128), jnp.bfloat16)
    inter[LEFT_PAIRS] = jnp.zeros((2, 128, 128), jnp.bfloat16)
    cumulated[RIGHT_PAIRS] = jnp.zeros((256, 128), jnp.float32)
    pl.semaphore_wait(barrier, 13 + jnp.where(fixed, 0, 1))
    Y_SEND, EY_SEND, MATE_SEND, XUP, XDOWN, ZUP, ZDOWN, E_SEND, LISTS_SEND = range(9)

    def remote(source, target, sender, receiver, device):
        pltpu.make_async_remote_copy(
            src_ref=source, dst_ref=target, send_sem=send.at[sender], recv_sem=receiver,
            device_id=device, device_id_type=MESH,
        ).start()

    def wait(ref, sem):
        pltpu.make_async_copy(ref, ref, sem).wait()

    def chunks(slot, count=1):
        return wave.at[pl.ds(2 * slot, 2 * count)]

    def pass_wave(slot, sender, device):
        remote(chunks(slot), chunks(slot), sender, wrecv.at[slot], device)

    def pass_mate(slot):
        remote(chunks(slot), chunks(slot), MATE_SEND, mate_recv, mate)

    def pass_env(slot, sender, device):
        remote(env.at[slot], env.at[slot], sender, erecv.at[slot], device)

    mine = xc * 8 + y

    @pl.when(fixed)
    def _():
        pltpu.make_async_copy(left_in, env.at[mine, 0], erecv.at[mine]).start()
        pltpu.make_async_copy(right_in, env.at[mine, 1], erecv.at[mine]).start()

    @pl.when(jnp.logical_not(fixed))
    def _():
        remote(left_in, env.at[mine, 0], E_SEND, erecv.at[mine], partner)
        remote(right_in, env.at[mine, 1], E_SEND, erecv.at[mine], partner)

    fetch.wait()
    for to in range(8):
        owner = (z // 2 * 8 + to) * 2 + z % 2
        for slot in range(2):
            index = picks[0, 2 * owner + slot]
            tile = tiles[jnp.maximum(index, 0)]
            outgoing[2 * to + slot] = jnp.where(index >= 0, tile, jnp.zeros_like(tile))

    own = z * 8 + y

    def shift(r):
        step = (r + 1) // 2
        return jnp.where(r % 2 == 1, step, 8 - step)

    def send_wave(r):
        to = (y + 8 - shift(r)) % 8
        remote(outgoing.at[pl.ds(2 * to, 2)], chunks(mine), Y_SEND, wrecv.at[mine], (z, x, to, c))

    def send_env(r):
        to = (y + 8 - shift(r)) % 8
        remote(env.at[own], env.at[own], EY_SEND, erecv.at[own], (z, x, to, c))

    here = outgoing.at[pl.ds(2 * y, 2)]
    pltpu.make_async_copy(here, chunks(mine), wrecv.at[mine]).start()
    for r in range(1, 5):
        send_wave(r)
    remote(here, chunks(mine), XUP, wrecv.at[mine], xup)
    remote(here, chunks(mine), XDOWN, wrecv.at[mine], xdown)
    remote(here, chunks(mine), MATE_SEND, mate_recv, mate)
    build_lists(left_tasks, right_tasks, lists_in)

    @pl.when(fixed)
    def _():
        pltpu.make_async_copy(lists_in, lists_vmem, lists_recv).start()

    @pl.when(jnp.logical_not(fixed))
    def _():
        remote(lists_in, lists_vmem, LISTS_SEND, lists_recv, partner)

    wait(env.at[own], erecv.at[own])
    for r in range(1, 5):
        send_env(r)

    def source(r):
        return (y + shift(r)) % 8

    def turn(i, carry):
        @pl.when(i < 3)
        def _():
            send_wave(i + 5)
            send_env(i + 5)

        @pl.when(i < 8)
        def _():
            yy = source(i)
            slot = xc * 8 + yy

            @pl.when(i > 0)
            def _():
                wait(chunks(slot), wrecv.at[slot])
                pass_wave(slot, XUP, xup)
                pass_wave(slot, XDOWN, xdown)
                pass_mate(slot)

            slot = z * 8 + yy

            @pl.when(i > 0)
            def _():
                wait(env.at[slot], erecv.at[slot])

            pass_env(slot, ZUP, zup)
            pass_env(slot, ZDOWN, zdown)

        @pl.when(jnp.logical_and(i >= 1, i < 9))
        def _():
            yy = source(i - 1)
            even = yy % 2 == 0
            low = (2 * ((x + 3) % 4) + c) * 8 + yy
            wait(chunks(low), wrecv.at[low])

            @pl.when(even)
            def _():
                pass_wave(low, XUP, xup)

            pass_mate(low)
            high = (2 * ((x + 1) % 4) + c) * 8 + yy
            wait(chunks(high), wrecv.at[high])

            @pl.when(jnp.logical_not(even))
            def _():
                pass_wave(high, XDOWN, xdown)

            pass_mate(high)
            low, high = ((z + 7) % 8) * 8 + yy, ((z + 1) % 8) * 8 + yy
            wait(env.at[low], erecv.at[low])
            pass_env(low, ZUP, zup)
            wait(env.at[high], erecv.at[high])
            pass_env(high, ZDOWN, zdown)

        @pl.when(jnp.logical_and(i >= 2, i < 10))
        def _():
            yy = source(i - 2)
            far = (2 * ((x + 2) % 4) + c) * 8 + yy
            wait(chunks(far), wrecv.at[far])
            pass_mate(far)
            low, high = ((z + 6) % 8) * 8 + yy, ((z + 2) % 8) * 8 + yy
            wait(env.at[low], erecv.at[low])
            pass_env(low, ZUP, zup)
            wait(env.at[high], erecv.at[high])
            pass_env(high, ZDOWN, zdown)

        @pl.when(jnp.logical_and(i >= 3, i < 11))
        def _():
            yy = source(i - 3)
            even = yy % 2 == 0
            low, high = ((z + 5) % 8) * 8 + yy, ((z + 3) % 8) * 8 + yy
            wait(env.at[low], erecv.at[low])

            @pl.when(even)
            def _():
                pass_env(low, ZUP, zup)

            wait(env.at[high], erecv.at[high])

            @pl.when(jnp.logical_not(even))
            def _():
                pass_env(high, ZDOWN, zdown)

        @pl.when(i >= 4)
        def _():
            far = ((z + 4) % 8) * 8 + source(i - 4)
            wait(env.at[far], erecv.at[far])

        return carry

    lax.fori_loop(0, 12, turn, 0)

    wait(lists_vmem, lists_recv)
    load = pltpu.make_async_copy(lists_vmem, lists, lists_recv)
    load.start()
    wait(chunks(mine), wrecv.at[mine])
    wait(chunks(0, 32), mate_recv)
    load.wait()

    def left_pair(p, total):
        one, two = lists[0, 2 * p], lists[0, 2 * p + 1]
        lhs = jnp.concatenate([env[(one >> 8) & 63, 0], env[(two >> 8) & 63, 0]], axis=1)
        rhs = jnp.concatenate(
            [
                jnp.concatenate([wave[one & 255, 0], wave[one & 255, 1]], axis=1),
                jnp.concatenate([wave[two & 255, 0], wave[two & 255, 1]], axis=1),
            ],
            axis=0,
        )
        product = jnp.dot(lhs, rhs, preferred_element_type=jnp.float32)
        total = product + total * (one >> 16).astype(jnp.float32)
        inter[p, 0] = total[:, :128].astype(jnp.bfloat16)
        inter[p, 1] = total[:, 128:].astype(jnp.bfloat16)
        return total

    lax.fori_loop(0, LEFT_PAIRS, left_pair, jnp.zeros((128, 256), jnp.float32), unroll=32)

    def right_pair(p, total):
        row, column = 1 + p // 64, 2 * (p % 64)
        one, two = lists[row, column], lists[row, column + 1]
        lhs = jnp.concatenate(
            [
                inter[(one >> 8) & 127].reshape(256, 128),
                inter[(two >> 8) & 127].reshape(256, 128),
            ],
            axis=1,
        )
        rhs = jnp.concatenate([env[one & 63, 1], env[two & 63, 1]], axis=0)
        product = jnp.dot(lhs, rhs, preferred_element_type=jnp.float32)
        total = product + total * (one >> 16).astype(jnp.float32)
        cumulated[p] = total
        return total

    lax.fori_loop(0, RIGHT_PAIRS, right_pair, jnp.zeros((256, 128), jnp.float32), unroll=34)

    def block(h):
        return pl.ds(TILES // STEPS * h, TILES // STEPS)

    def to_mate(h):
        return pltpu.make_async_remote_copy(
            src_ref=partial.at[1 - c, :, block(h)], dst_ref=theirs.at[:, block(h)],
            send_sem=theirs_send.at[h], recv_sem=theirs_recv.at[h],
            device_id=mate, device_id_type=MESH,
        )

    def to_chip(h, k):
        return pltpu.make_async_remote_copy(
            src_ref=pair.at[(x + k) % 4, block(h)], dst_ref=parts.at[k - 1, block(h)],
            send_sem=part_send.at[4 * h + k], recv_sem=recv.at[4 * h + k],
            device_id=lane[k - 1], device_id_type=MESH,
        )

    for h in range(STEPS):
        for k in range(TILES // STEPS * h, TILES // STEPS * (h + 1)):
            tile = cumulated[lists[4, k]].reshape(2, 8, 16, 128)
            for t in range(8):
                partial[t % 2, t // 2, k] = tile[:, t]
        to_mate(h).start()
    for h in range(STEPS):
        to_mate(h).wait_recv()
        pair[:, block(h)] = (partial[c, :, block(h)] + theirs[:, block(h)]).astype(jnp.bfloat16)
        for k in (2, 1, 3):
            to_chip(h, k).start()
    for h in range(STEPS):
        total = partial[c, x, block(h)] + theirs[x, block(h)]
        for k in (1, 2, 3):
            to_chip(h, k).wait_recv()
            total += parts[k - 1, block(h)].astype(jnp.float32)
        result[block(h)] = total.astype(jnp.bfloat16)

        @pl.when(fixed)
        def _():
            pltpu.make_async_copy(result.at[block(h)], out.at[block(h)], last_recv.at[h]).start()

        @pl.when(jnp.logical_not(fixed))
        def _():
            pltpu.make_async_remote_copy(
                src_ref=result.at[block(h)], dst_ref=out.at[block(h)],
                send_sem=last_send.at[h], recv_sem=last_recv.at[h],
                device_id=partner, device_id_type=MESH,
            ).start()

    wait(chunks(0, 7), send.at[Y_SEND])
    wait(env.at[pl.ds(0, 7)], send.at[EY_SEND])
    wait(chunks(0, 32), send.at[MATE_SEND])
    wait(chunks(0, 12), send.at[XUP])
    wait(chunks(0, 12), send.at[XDOWN])
    wait(env.at[pl.ds(0, 28)], send.at[ZUP])
    wait(env.at[pl.ds(0, 28)], send.at[ZDOWN])
    for h in range(STEPS):
        to_mate(h).wait_send()
        for k in (1, 2, 3):
            to_chip(h, k).wait_send()

    @pl.when(jnp.logical_not(fixed))
    def _():
        wait(env.at[0], send.at[E_SEND])
        wait(lists_vmem, send.at[LISTS_SEND])
        for h in range(STEPS):
            wait(result.at[pl.ds(0, TILES // STEPS)], last_send.at[h])

    for h in range(STEPS):
        wait(result.at[pl.ds(0, TILES // STEPS)], last_recv.at[h])


def main(*operands):
    return pl.pallas_call(
        main_kernel,
        out_shape=jax.ShapeDtypeStruct((TILES, 2, 16, 128), jnp.bfloat16),
        in_specs=[ANY, SMEM, ANY, ANY, VMEM, VMEM],
        out_specs=VMEM,
        scratch_shapes=[
            pltpu.VMEM((16, 2, 128, 128), jnp.bfloat16),
            pltpu.VMEM((16, 2, 128, 128), jnp.bfloat16),
            pltpu.VMEM((8, 128), jnp.int32),
            pltpu.VMEM((8, 128), jnp.int32),
            pltpu.SMEM((8, 128), jnp.int32),
            pltpu.VMEM((129, 2, 128, 128), jnp.bfloat16),
            pltpu.VMEM((64, 2, 128, 128), jnp.bfloat16),
            pltpu.VMEM((LEFT_PAIRS + 1, 2, 128, 128), jnp.bfloat16),
            pltpu.VMEM((RIGHT_PAIRS + 1, 256, 128), jnp.float32),
            pltpu.VMEM((2, 4, TILES, 2, 16, 128), jnp.float32),
            pltpu.VMEM((4, TILES, 2, 16, 128), jnp.float32),
            pltpu.VMEM((4, TILES, 2, 16, 128), jnp.bfloat16),
            pltpu.VMEM((3, TILES, 2, 16, 128), jnp.bfloat16),
            pltpu.VMEM((TILES, 2, 16, 128), jnp.bfloat16),
            pltpu.SemaphoreType.DMA((64,)),
            pltpu.SemaphoreType.DMA((64,)),
            pltpu.SemaphoreType.DMA,
            pltpu.SemaphoreType.DMA,
            pltpu.SemaphoreType.DMA((9,)),
            pltpu.SemaphoreType.DMA((STEPS,)),
            pltpu.SemaphoreType.DMA((STEPS,)),
            pltpu.SemaphoreType.DMA((4 * STEPS,)),
            pltpu.SemaphoreType.DMA((4 * STEPS,)),
            pltpu.SemaphoreType.DMA((STEPS,)),
            pltpu.SemaphoreType.DMA((STEPS,)),
            pltpu.SemaphoreType.DMA,
        ],
        compiler_params=pltpu.CompilerParams(
            collective_id=0, has_side_effects=True, vmem_limit_bytes=60 << 20
        ),
        name="main",
    )(*operands)


def shards(wave_tiles, left_env, right_env, send_list, left_tasks, right_tasks):
    rows = main(
        wave_tiles,
        send_list,
        left_env[0, 0],
        right_env[0, 0],
        jnp.transpose(left_tasks[0], (2, 0, 1)),
        jnp.transpose(right_tasks[0], (2, 0, 1)),
    )
    return rows.astype(jnp.float32)


def solution(mesh):
    fine = Mesh(mesh.devices.reshape(8, 4, 8, 2), AXES)
    sector = ("x", "y", "core")
    in_specs = (
        P(sector, None, None, None),
        P("z", sector, None, None),
        P("z", sector, None, None),
        P(sector, None),
        P("z", sector, None, None),
        P("z", sector, None, None),
    )
    out_specs = P(sector, None, "z", None)
    return jax.shard_map(shards, mesh=fine, in_specs=in_specs, out_specs=out_specs, check_vma=False)
```
